512 devices in a mesh: aux: 32 (over x_lo, y, core), occ: 16 (over z, x_hi).
Axes of the slice: x: 4 (x_hi: 2, x_lo: 2; x = x_hi * 2 + x_lo), y: 8, z: 8, core: 2. Of those that a mesh axis runs over, the one named last changes fastest.
Arguments:
- half_ints: bfloat16 [2048, 32, 576], P(('aux', 'occ')), may hold values from -6 to 6
- vir_coef: bfloat16 [576, 512], replicated, may hold values from -0.03125 to 0.03125
- occ_energy: float32 [32], replicated, may hold values from -2 to -0.5
- vir_energy: float32 [512], replicated, may hold values from 0.2 to 3
Outputs:
- density: float32 [2048, 32, 512], P('occ', 'aux')
The draws below stay inside these ranges and needn't reach their ends.
All inputs are finite; a program needn't handle non-finite values.
Results may differ from the reference program's by a relative error of at most 0.0032.
Values may be sent and summed in bfloat16 or wider, within the bound.
No kernel may reach another device: no remote copies, remote signals or barrier semaphores. Data moves between devices by JAX's collectives and lax.ppermute only.
A program may use at most 64 MiB of HBM per device.

```python
import jax
import jax.numpy as jnp
from jax import lax

NAUX = 2048
NBF = 576
NVIR = 512
NB = 32


def level_of(own_key, dims, pieces, smallest, high):
    level = 1.0
    for axis_at, parts in pieces:
        steps = jax.random.uniform(jax.random.fold_in(jax.random.fold_in(own_key, 6), axis_at), (parts,), jnp.float32, smallest / len(pieces), high / len(pieces))
        level = level * jnp.repeat(jnp.exp(steps), dims[axis_at] // parts).reshape((-1,) + (1,) * (len(dims) - 1 - axis_at))
    return level


def centred(key, shape, scale, reach, split=(), kind=jnp.bfloat16):
    drawn = jax.random.normal(key, shape, jnp.float32) * scale
    if len(split) > 0:
        drawn = level_of(key, shape, split, -0.22, 0.18) * drawn
    return jnp.clip(drawn, min=-reach, max=reach).astype(kind)


def setup_inputs(seed: int = 0) -> dict:
    arg_keys = jax.random.split(jax.random.key(seed), 5)
    half_ints = centred(arg_keys[0], (NAUX, NB, NBF), 1.0, 6.0, ((0, 512),))
    vir_coef = centred(arg_keys[1], (NBF, NVIR), (NBF * 64) ** -0.5, 0.03125)
    occ_energy = jnp.clip(jax.random.uniform(arg_keys[2], (NB,), jnp.float32, -2.0, -0.5), -2.0, -0.5)
    vir_energy = jnp.clip(jax.random.uniform(arg_keys[3], (NVIR,), jnp.float32, 0.2, 3.0), 0.2, 3.0)
    return dict(half_ints=half_ints, vir_coef=vir_coef, occ_energy=occ_energy, vir_energy=vir_energy)


def reference(half_ints, vir_coef, occ_energy, vir_energy):
    flattened = half_ints.reshape(NAUX * NB, NBF)
    three_index = jnp.dot(flattened, vir_coef, preferred_element_type=jnp.float32).astype(jnp.bfloat16)
    ints_all = three_index.reshape(NAUX, NB, NVIR)
    wide_right = three_index.reshape(NAUX, NB * NVIR).astype(jnp.float32)

    def one_occupied(index):
        left_side = lax.dynamic_index_in_dim(ints_all, index, 1, keepdims=False).astype(jnp.float32)
        coulomb = jnp.dot(left_side.T, wide_right).reshape(NVIR, NB, NVIR)
        swapped = coulomb.transpose(2, 1, 0)
        occ_first = lax.dynamic_index_in_dim(occ_energy, index, 0, keepdims=False)
        denominator = vir_energy[:, None, None] + vir_energy[None, None, :] - occ_first - occ_energy[None, :, None]
        amplitude = ((2.0 * coulomb - swapped) / denominator).astype(jnp.bfloat16).reshape(NVIR, NB * NVIR)
        return jnp.dot(wide_right, amplitude.astype(jnp.float32).T)

    stacked = lax.map(one_occupied, jnp.arange(NB, dtype=jnp.int32))
    return stacked.transpose(1, 0, 2)
```

```python
import functools

import jax
import jax.numpy as jnp
from jax import lax
from jax.experimental import pallas as pl
from jax.experimental.pallas import tpu as pltpu
from jax.sharding import Mesh
from jax.sharding import PartitionSpec as P


XL, Y, C, Z, XH = 2, 8, 2, 8, 2
AXES = ("xl", "y", "c", "z", "xh")
MIB = 1 << 20
VMEM = pl.BlockSpec(memory_space=pltpu.VMEM)
SMEM = pl.BlockSpec(memory_space=pltpu.SMEM)


def exact_rows(source_row, count, rows):
    wanted = lax.broadcasted_iota(jnp.int32, (count, count), 1)
    selection = (wanted == source_row).astype(jnp.bfloat16)
    return jnp.dot(selection, rows, preferred_element_type=jnp.float32).astype(jnp.bfloat16)


def three_index_kernel(where, half_ref, coef_ref, out_ref):
    row = lax.broadcasted_iota(jnp.int32, (128, 128), 0)
    local, pick, xh, z = row % 4, (row // 4) % 2, (row // 8) % 2, row // 16
    core = where[0]
    orbital = 2 * (xh * Z + z) + (pick + core) % 2
    ordered = exact_rows(local * 32 + orbital, 128, half_ref[...])
    ints = jnp.dot(ordered, coef_ref[...], preferred_element_type=jnp.float32).astype(jnp.bfloat16)
    out_ref[0:128, :] = ints
    out_ref[128:256, :] = ints


def reorder_kernel(in_ref, out_ref):
    row = lax.broadcasted_iota(jnp.int32, (256, 256), 0)
    local, device, pick = row % 4, (row // 4) % 32, row // 128
    out_ref[...] = exact_rows(device * 8 + pick * 4 + local, 256, in_ref[...])


def density_kernel(where, occ_ref, left_ref, own_ref, other_ref, vir_ref, out_ref, coulomb, total):
    down = jnp.broadcast_to(vir_ref[...], (512, 512))
    total[...] = down.T + down
    coulomb[...] = jnp.zeros_like(coulomb)

    @pl.loop(0, Y)
    def _(block):
        left = left_ref[block].T
        for pick in range(2):
            right = jnp.concatenate(
                [own_ref[block, 128 * pick : 128 * pick + 128, :], other_ref[block, 128 - 128 * pick : 256 - 128 * pick, :]]
            )
            coulomb[pick] += jnp.dot(left, right, preferred_element_type=jnp.float32)

    amplitudes = []
    for pick in range(2):
        plain = coulomb[pick]
        flipped = plain.T
        denominator = total[...] - occ_ref[where[0]] - occ_ref[where[1 + pick]]
        amplitudes.append(((2.0 * flipped - plain) / denominator).astype(jnp.bfloat16))
    stacked = [jnp.concatenate(amplitudes), jnp.concatenate(amplitudes[::-1])]
    for part, (source, amplitude) in enumerate(zip((own_ref, other_ref), stacked)):
        coulomb_like = amplitude

        @pl.loop(0, Y)
        def _(block):
            right = jnp.concatenate([source[block, 0:128, :], source[block, 128:256, :]], axis=1)
            term = jnp.dot(right, coulomb_like, preferred_element_type=jnp.float32).astype(jnp.bfloat16)
            for xl in range(XL):
                out_ref[xl * Y + block, 64 * part : 64 * part + 64, :] = term[64 * xl : 64 * xl + 64]


def call(kernel, shape, specs, scratch=(), flops=0):
    return pl.pallas_call(
        kernel,
        out_shape=jax.ShapeDtypeStruct(shape, jnp.bfloat16),
        in_specs=specs,
        out_specs=VMEM,
        scratch_shapes=list(scratch),
        compiler_params=pltpu.CompilerParams(vmem_limit_bytes=24 * MIB),
        cost_estimate=pl.CostEstimate(flops=flops, bytes_accessed=2 * MIB, transcendentals=0),
    )


def transposed(other_core):
    pairs = []
    for source in range(XL * Y * C * Z * XH):
        rest, xh = divmod(source, XH)
        rest, z = divmod(rest, Z)
        rest, c = divmod(rest, C)
        xl, y = divmod(rest, Y)
        core = 1 - c if other_core else c
        pairs.append((source, (((xh * Y + z) * C + core) * Z + y) * XH + xl))
    return pairs


def spread(rows, axis):
    copies = jnp.broadcast_to(rows[None], (8, *rows.shape))
    return lax.all_to_all(copies, axis, split_axis=0, concat_axis=0, tiled=True)


def body(half_ints, vir_coef, occ_energy, vir_energy):
    xl, y, c, z, xh = (lax.axis_index(a) for a in AXES)
    left_index = 2 * (xl * Y + y) + c
    pair = 2 * (xh * Z + z)
    ints = call(three_index_kernel, (256, 512), [SMEM, VMEM, VMEM])(
        jnp.reshape(c, (1,)), half_ints.reshape(128, 576), vir_coef
    )
    sent = lax.all_to_all(ints.reshape(32, 8, 512), ("xl", "z", "xh"), split_axis=0, concat_axis=0, tiled=True)
    pairs = call(reorder_kernel, (256, 512), [VMEM])(sent.reshape(256, 512))
    left_own = lax.ppermute(pairs[:128], AXES, transposed(False))
    left_other = lax.ppermute(pairs[128:], AXES, transposed(True))
    own = spread(pairs, "y")
    left = spread(jnp.concatenate([left_own, left_other]), "z")
    other = lax.ppermute(own, "c", [(0, 1), (1, 0)])
    where = jnp.stack([left_index, pair + c, pair + 1 - c])
    partial = call(
        density_kernel,
        (16, 128, 512),
        [SMEM, SMEM, VMEM, VMEM, VMEM, VMEM],
        [pltpu.VMEM((2, 512, 512), jnp.float32), pltpu.VMEM((512, 512), jnp.float32)],
        flops=4 * 512 * 1024 * 2048,
    )(where, occ_energy, left, own, other, vir_energy.reshape(1, 512))
    shares = lax.all_to_all(partial, ("z", "xh"), split_axis=0, concat_axis=0, tiled=True)
    summed = jnp.sum(shares.astype(jnp.float32), axis=0)
    ordered = jnp.where(c == 0, summed, jnp.concatenate([summed[64:], summed[:64]]))
    return ordered.reshape(128, 1, 512)


def solution(mesh):
    fine = Mesh(mesh.devices.reshape(XL, Y, C, Z, XH), AXES)
    return jax.shard_map(
        body,
        mesh=fine,
        in_specs=(P(AXES, None, None), P(), P(), P()),
        out_specs=P(("z", "xh"), ("xl", "y", "c"), None),
        check_vma=False,
    )
```

```python
import functools

import jax
import jax.numpy as jnp
from jax import lax
from jax.experimental import pallas as pl
from jax.experimental.pallas import tpu as pltpu
from jax.sharding import Mesh
from jax.sharding import PartitionSpec as P


XL, Y, C, Z, XH = 2, 8, 2, 8, 2
AXES = ("xl", "y", "c", "z", "xh")
MIB = 1 << 20
VMEM = pl.BlockSpec(memory_space=pltpu.VMEM)
SMEM = pl.BlockSpec(memory_space=pltpu.SMEM)


def exact_rows(source_row, count, rows):
    wanted = lax.broadcasted_iota(jnp.int32, (count, count), 1)
    selection = (wanted == source_row).astype(jnp.bfloat16)
    return jnp.dot(selection, rows, preferred_element_type=jnp.float32).astype(jnp.bfloat16)


def three_index_kernel(where, half_ref, coef_ref, out_ref):
    row = lax.broadcasted_iota(jnp.int32, (128, 128), 0)
    local, pick, xh, z = row % 4, (row // 4) % 2, (row // 8) % 2, row // 16
    core = where[0]
    orbital = 2 * (xh * Z + z) + (pick + core) % 2
    ordered = exact_rows(local * 32 + orbital, 128, half_ref[...])
    ints = jnp.dot(ordered, coef_ref[...], preferred_element_type=jnp.float32).astype(jnp.bfloat16)
    out_ref[0:128, :] = ints
    out_ref[128:256, :] = ints


def reorder_kernel(in_ref, out_ref):
    row = lax.broadcasted_iota(jnp.int32, (256, 256), 0)
    local, device, pick = row % 4, (row // 4) % 32, row // 128
    out_ref[...] = exact_rows(device * 8 + pick * 4 + local, 256, in_ref[...])


def density_kernel(where, occ_ref, first, second, first_other, second_other, vir_ref, out_ref, coulomb, total):
    @pl.when(where[3] == 0)
    def _():
        density(where, occ_ref, second, first, second_other, vir_ref, out_ref, coulomb, total)

    @pl.when(where[3] == 1)
    def _():
        density(where, occ_ref, first, second, first_other, vir_ref, out_ref, coulomb, total)


def density(where, occ_ref, left_ref, own_ref, other_ref, vir_ref, out_ref, coulomb, total):
    down = jnp.broadcast_to(vir_ref[...], (512, 512))
    total[...] = down.T + down
    coulomb[...] = jnp.zeros_like(coulomb)

    @pl.loop(0, Y)
    def _(block):
        left = left_ref[block].T
        for pick in range(2):
            right = jnp.concatenate(
                [own_ref[block, 128 * pick : 128 * pick + 128, :], other_ref[block, 128 - 128 * pick : 256 - 128 * pick, :]]
            )
            coulomb[pick] += jnp.dot(left, right, preferred_element_type=jnp.float32)

    amplitudes = []
    for pick in range(2):
        plain = coulomb[pick]
        flipped = plain.T
        denominator = total[...] - occ_ref[where[0]] - occ_ref[where[1 + pick]]
        amplitudes.append(((2.0 * flipped - plain) / denominator).astype(jnp.bfloat16))
    stacked = [jnp.concatenate(amplitudes), jnp.concatenate(amplitudes[::-1])]
    for part, (source, amplitude) in enumerate(zip((own_ref, other_ref), stacked)):
        coulomb_like = amplitude

        @pl.loop(0, Y)
        def _(block):
            right = jnp.concatenate([source[block, 0:128, :], source[block, 128:256, :]], axis=1)
            term = jnp.dot(right, coulomb_like, preferred_element_type=jnp.float32).astype(jnp.bfloat16)
            for xl in range(XL):
                out_ref[xl * Y + block, 64 * part : 64 * part + 64, :] = term[64 * xl : 64 * xl + 64]


def call(kernel, shape, specs, scratch=(), flops=0):
    return pl.pallas_call(
        kernel,
        out_shape=jax.ShapeDtypeStruct(shape, jnp.bfloat16),
        in_specs=specs,
        out_specs=VMEM,
        scratch_shapes=list(scratch),
        compiler_params=pltpu.CompilerParams(vmem_limit_bytes=24 * MIB),
        cost_estimate=pl.CostEstimate(flops=flops, bytes_accessed=2 * MIB, transcendentals=0),
    )


def transposed(other_core):
    pairs = []
    for source in range(XL * Y * C * Z * XH):
        rest, xh = divmod(source, XH)
        rest, z = divmod(rest, Z)
        rest, c = divmod(rest, C)
        xl, y = divmod(rest, Y)
        core = 1 - c if other_core else c
        pairs.append((source, device(xh, z, core, y, xl)))
    return pairs


def device(xl, y, c, z, xh):
    return (((xl * Y + y) * C + c) * Z + z) * XH + xh


def lines(along_y):
    groups = []
    for xl in range(XL):
        for xh in range(XH):
            for at in range(8):
                groups.append([device(xl, y, along_y, at, xh) for y in range(Y)])
                groups.append([device(xl, at, 1 - along_y, z, xh) for z in range(Z)])
    return groups


def spread(rows, along_y):
    copies = jnp.broadcast_to(rows[None], (8, *rows.shape))
    return lax.all_to_all(
        copies, AXES, split_axis=0, concat_axis=0, axis_index_groups=lines(along_y), tiled=True
    )


def to_core(rows, core):
    pairs = []
    for chip in range(XL * Y * Z * XH):
        rest, line = divmod(chip, Z * XH)
        first = rest * C * Z * XH + line
        at = (first, first + Z * XH)
        pairs.append((at[1 - core], at[core]))
    return lax.ppermute(rows, AXES, pairs)


def body(half_ints, vir_coef, occ_energy, vir_energy):
    xl, y, c, z, xh = (lax.axis_index(a) for a in AXES)
    left_index = 2 * (xl * Y + y) + c
    pair = 2 * (xh * Z + z)
    ints = call(three_index_kernel, (256, 512), [SMEM, VMEM, VMEM])(
        jnp.reshape(c, (1,)), half_ints.reshape(128, 576), vir_coef
    )
    sent = lax.all_to_all(ints.reshape(32, 8, 512), ("xl", "z", "xh"), split_axis=0, concat_axis=0, tiled=True)
    pairs = call(reorder_kernel, (256, 512), [VMEM])(sent.reshape(256, 512))
    left_own = lax.ppermute(pairs[:128], AXES, transposed(False))
    left_other = lax.ppermute(pairs[128:], AXES, transposed(True))
    lefts = jnp.concatenate([left_own, left_other])
    first = spread(jnp.where(c == 0, pairs, lefts), 0)
    second = spread(jnp.where(c == 0, lefts, pairs), 1)
    first_other = to_core(first, 1)
    second_other = to_core(second, 0)
    where = jnp.stack([left_index, pair + c, pair + 1 - c, c])
    partial = call(
        density_kernel,
        (16, 128, 512),
        [SMEM, SMEM, VMEM, VMEM, VMEM, VMEM, VMEM],
        [pltpu.VMEM((2, 512, 512), jnp.float32), pltpu.VMEM((512, 512), jnp.float32)],
        flops=4 * 512 * 1024 * 2048,
    )(where, occ_energy, first, second, first_other, second_other, vir_energy.reshape(1, 512))
    shares = lax.all_to_all(partial, ("z", "xh"), split_axis=0, concat_axis=0, tiled=True)
    summed = jnp.sum(shares.astype(jnp.float32), axis=0)
    ordered = jnp.where(c == 0, summed, jnp.concatenate([summed[64:], summed[:64]]))
    return ordered.reshape(128, 1, 512)


def solution(mesh):
    fine = Mesh(mesh.devices.reshape(XL, Y, C, Z, XH), AXES)
    return jax.shard_map(
        body,
        mesh=fine,
        in_specs=(P(AXES, None, None), P(), P(), P()),
        out_specs=P(("z", "xh"), ("xl", "y", "c"), None),
        check_vma=False,
    )
```

```python
import jax
import jax.numpy as jnp
from jax import lax
from jax.experimental import pallas as pl
from jax.experimental.pallas import tpu as pltpu
from jax.sharding import Mesh
from jax.sharding import PartitionSpec as P


AXES = ("xl", "y4", "yb", "c", "z4", "zb", "xh")
SIZES = (2, 4, 2, 2, 4, 2, 2)
COMPACT = ("xl", "yb", "xh", "zb")
WIDE = ("y4", "z4")
MIB = 1 << 20
VMEM = pl.BlockSpec(memory_space=pltpu.VMEM)
SMEM = pl.BlockSpec(memory_space=pltpu.SMEM)


def exact_rows(source_row, rows):
    wanted = lax.broadcasted_iota(jnp.int32, source_row.shape, 1)
    selection = (wanted == source_row).astype(jnp.bfloat16)
    return jnp.dot(selection, rows, preferred_element_type=jnp.float32).astype(jnp.bfloat16)


def left_orbital(y4, z4, c):
    return ((z4 // 2) * 8 + y4 * 2 + z4 % 2) * 2 + c


def three_index_kernel(half_ref, coef_ref, left_ref, right_ref):
    row = lax.broadcasted_iota(jnp.int32, (128, 128), 0)
    local, orbital = row % 4, row // 4
    target = left_orbital(orbital // 8, (orbital // 2) % 4, orbital % 2)
    ints = jnp.dot(half_ref[...], coef_ref[...], preferred_element_type=jnp.float32).astype(jnp.bfloat16)
    left_ref[...] = exact_rows(local * 32 + target, ints)
    right_ref[...] = exact_rows(local * 32 + orbital, ints)


def density_kernel(where, occ_ref, left_ref, own_ref, other_ref, vir_ref, out_ref, coulomb, total):
    core = where[3]
    down = jnp.broadcast_to(vir_ref[...], (512, 512))
    total[...] = down.T + down
    coulomb[...] = jnp.zeros_like(coulomb)

    def block(ref, ref_core, y4, z4):
        return ref[jnp.where(ref_core == 0, z4 * 4 + y4, y4 * 4 + z4)]

    def rows(ref, ref_core, y4):
        return jnp.concatenate([block(ref, ref_core, y4, z4) for z4 in range(4)])

    @pl.loop(0, 4)
    def _(y4):
        left = jnp.concatenate([left_ref[:, y4 * 4 + z4].reshape(128, 512) for z4 in range(4)]).T
        coulomb[0] += jnp.dot(left, rows(own_ref, core, y4), preferred_element_type=jnp.float32)
        coulomb[1] += jnp.dot(left, rows(other_ref, 1 - core, y4), preferred_element_type=jnp.float32)

    amplitudes = []
    for pick in range(2):
        plain = coulomb[pick]
        flipped = plain.T
        denominator = total[...] - occ_ref[where[0]] - occ_ref[where[1 + pick]]
        amplitudes.append(((2.0 * flipped - plain) / denominator).astype(jnp.bfloat16))

    @pl.loop(0, 4)
    def _(y4):
        term = jnp.dot(rows(own_ref, core, y4), amplitudes[0], preferred_element_type=jnp.float32)
        term += jnp.dot(rows(other_ref, 1 - core, y4), amplitudes[1], preferred_element_type=jnp.float32)
        term = term.astype(jnp.bfloat16)
        for z4 in range(4):
            for xl in range(2):
                for yb in range(2):
                    share = xl * 8 + (y4 // 2) * 4 + yb * 2 + y4 % 2
                    at = z4 * 128 + xl * 64 + yb * 32
                    out_ref[share, z4 * 32 : z4 * 32 + 32, :] = term[at : at + 32]


def call(kernel, shapes, specs, scratch=(), flops=0):
    return pl.pallas_call(
        kernel,
        out_shape=[jax.ShapeDtypeStruct(shape, jnp.bfloat16) for shape in shapes],
        in_specs=specs,
        out_specs=[VMEM] * len(shapes),
        scratch_shapes=list(scratch),
        compiler_params=pltpu.CompilerParams(vmem_limit_bytes=24 * MIB),
        cost_estimate=pl.CostEstimate(flops=flops, bytes_accessed=2 * MIB, transcendentals=0),
    )


def device(**at):
    index = 0
    for name, size in zip(AXES, SIZES):
        index = index * size + at[name]
    return index


def places():
    for index in range(512):
        at, rest = {}, index
        for name, size in zip(AXES[::-1], SIZES[::-1]):
            rest, at[name] = divmod(rest, size)
        yield index, at


def lines(core_along_y):
    groups = []
    for _, at in places():
        axis = "y4" if at["c"] == core_along_y else "z4"
        if at[axis] == 0:
            groups.append([device(**{**at, axis: k}) for k in range(4)])
    return groups


def spread(rows, count, axes, groups=None):
    copies = jnp.broadcast_to(rows[None], (count, *rows.shape))
    return lax.all_to_all(copies, axes, split_axis=0, concat_axis=0, axis_index_groups=groups, tiled=True)


def to_place():
    return [
        (index, device(**{**at, "xl": at["z4"] // 2, "yb": at["z4"] % 2, "z4": at["xl"] * 2 + at["yb"]}))
        for index, at in places()
    ]


def body(half_ints, vir_coef, occ_energy, vir_energy):
    xl, y4, yb, c, z4, zb, xh = (lax.axis_index(a) for a in AXES)
    pair = (((xl * 2 + yb) * 2 + xh) * 2 + zb) * 2
    where = jnp.stack([left_orbital(y4, z4, c), pair + c, pair + 1 - c, c])
    to_left, to_right = call(three_index_kernel, [(128, 512)] * 2, [VMEM, VMEM])(half_ints.reshape(128, 576), vir_coef)

    def exchange(rows, axes):
        return lax.all_to_all(rows.reshape(32, 4, 512), axes, split_axis=0, concat_axis=0, tiled=True).reshape(128, 512)

    right = exchange(to_right, (*COMPACT, "c"))
    line = spread(right, 4, AXES, lines(0)).reshape(512, 512)
    own = spread(line, 4, AXES, lines(1)).reshape(16, 128, 512)
    other = lax.ppermute(own, "c", [(0, 1), (1, 0)])
    left = spread(exchange(to_left, (*WIDE, "c")), 16, COMPACT)
    (partial,) = call(
        density_kernel,
        [(16, 128, 512)],
        [SMEM, SMEM, VMEM, VMEM, VMEM, VMEM],
        [pltpu.VMEM((2, 512, 512), jnp.float32), pltpu.VMEM((512, 512), jnp.float32)],
        flops=4 * 512 * 1024 * 2048,
    )(where, occ_energy, left.reshape(16, 16, 8, 512), own, other, vir_energy.reshape(1, 512))
    shares = lax.all_to_all(partial, COMPACT, split_axis=0, concat_axis=0, tiled=True)
    summed = jnp.sum(shares.astype(jnp.float32), axis=0)
    ordered = summed.reshape(4, 2, 2, 2, 4, 512).transpose(3, 0, 2, 1, 4, 5).reshape(128, 512)
    return lax.ppermute(ordered, AXES, to_place()).reshape(128, 1, 512)


def solution(mesh):
    fine = Mesh(mesh.devices.reshape(SIZES), AXES)
    return jax.shard_map(
        body,
        mesh=fine,
        in_specs=(P(AXES, None, None), P(), P(), P()),
        out_specs=P(("z4", "zb", "xh"), ("xl", "y4", "yb", "c"), None),
        check_vma=False,
    )
```

```python
import jax
import jax.numpy as jnp
from jax import lax
from jax.experimental import pallas as pl
from jax.experimental.pallas import tpu as pltpu
from jax.sharding import Mesh
from jax.sharding import PartitionSpec as P


AXES = ("xl", "y4", "yb", "c", "z4", "zb", "xh")
SIZES = (2, 4, 2, 2, 4, 2, 2)
COMPACT = ("xl", "yb", "xh", "zb")
MIB = 1 << 20
VMEM = pl.BlockSpec(memory_space=pltpu.VMEM)
SMEM = pl.BlockSpec(memory_space=pltpu.SMEM)


def exact_rows(source_row, rows):
    wanted = lax.broadcasted_iota(jnp.int32, source_row.shape, 1)
    selection = (wanted == source_row).astype(jnp.bfloat16)
    return jnp.dot(selection, rows, preferred_element_type=jnp.float32).astype(jnp.bfloat16)


def left_orbital(y4, z4, c):
    return ((z4 // 2) * 8 + y4 * 2 + z4 % 2) * 2 + c


def three_index_kernel(where, half_ref, coef_ref, keep_ref, give_ref):
    row = lax.broadcasted_iota(jnp.int32, (128, 128), 0)
    local, pair, pick = row % 4, (row // 4) % 16, row // 64
    ints = jnp.dot(half_ref[...], coef_ref[...], preferred_element_type=jnp.float32).astype(jnp.bfloat16)
    ordered = exact_rows(local * 32 + 2 * pair + (pick + where[3]) % 2, ints)
    keep_ref[...] = ordered[:64]
    give_ref[...] = ordered[64:]


def order_kernel(where, keep_ref, got_ref, left_ref, right_ref):
    core = where[3]
    rows = jnp.concatenate([keep_ref[...], got_ref[...]])
    row = lax.broadcasted_iota(jnp.int32, (128, 128), 0)
    local, first, second = row % 4 + 64 * ((row // 4 + core) % 2), row // 32, (row // 8) % 4
    y4, z4 = jnp.where(core == 0, first, second), jnp.where(core == 0, second, first)
    left_ref[...] = exact_rows(left_orbital(y4, z4, 0) // 2 * 4 + local, rows)
    right_ref[...] = exact_rows(row // 8 * 4 + local, rows)


def first_stage_kernel(right_ref, left_ref, out_ref):
    for target in range(4):
        out_ref[target, 0:128, :] = right_ref[...]
        out_ref[target, 128:160, :] = left_ref[32 * target : 32 * target + 32, :]


def second_stage_kernel(in_ref, out_ref):
    for target in range(4):
        for source in range(4):
            out_ref[target, 128 * source : 128 * source + 128, :] = in_ref[source, 0:128, :]
            at = 128 + 8 * target
            out_ref[target, 512 + 8 * source : 520 + 8 * source, :] = in_ref[source, at : at + 8, :]


def density_kernel(where, occ_ref, left_ref, own_ref, other_ref, vir_ref, out_ref, coulomb, total):
    core = where[3]
    down = jnp.broadcast_to(vir_ref[...], (512, 512))
    total[...] = down.T + down
    coulomb[...] = jnp.zeros_like(coulomb)

    def own(second):
        return own_ref[second, 0:512, :]

    def other(second):
        at = pl.ds(pl.multiple_of(second * 128, 128), 128)
        return jnp.concatenate([other_ref[first, at, :] for first in range(4)])

    @pl.loop(0, 4)
    def _(second):
        left = jnp.concatenate([left_ref[:, second * 4 + first].reshape(128, 512) for first in range(4)]).T
        coulomb[0] += jnp.dot(left, own(second), preferred_element_type=jnp.float32)
        coulomb[1] += jnp.dot(left, other(second), preferred_element_type=jnp.float32)

    amplitudes = []
    for pick in range(2):
        plain = coulomb[pick]
        flipped = plain.T
        denominator = total[...] - occ_ref[where[0]] - occ_ref[where[1 + pick]]
        amplitudes.append(((2.0 * flipped - plain) / denominator).astype(jnp.bfloat16))

    @pl.loop(0, 4)
    def _(second):
        term = jnp.dot(own(second), amplitudes[0], preferred_element_type=jnp.float32)
        term += jnp.dot(other(second), amplitudes[1], preferred_element_type=jnp.float32)
        term = term.astype(jnp.bfloat16)
        for first in range(4):
            y4, z4 = jnp.where(core == 0, first, second), jnp.where(core == 0, second, first)
            for xl in range(2):
                for yb in range(2):
                    share = xl * 8 + (y4 // 2) * 4 + yb * 2 + y4 % 2
                    at = first * 128 + xl * 64 + yb * 32
                    out_ref[share, pl.ds(pl.multiple_of(z4 * 32, 32), 32), :] = term[at : at + 32]


def call(kernel, shapes, specs, scratch=(), flops=0):
    return pl.pallas_call(
        kernel,
        out_shape=[jax.ShapeDtypeStruct(shape, jnp.bfloat16) for shape in shapes],
        in_specs=specs,
        out_specs=[VMEM] * len(shapes),
        scratch_shapes=list(scratch),
        compiler_params=pltpu.CompilerParams(vmem_limit_bytes=24 * MIB),
        cost_estimate=pl.CostEstimate(flops=flops, bytes_accessed=2 * MIB, transcendentals=0),
    )


def device(**at):
    index = 0
    for name, size in zip(AXES, SIZES):
        index = index * size + at[name]
    return index


def places():
    for index in range(512):
        at, rest = {}, index
        for name, size in zip(AXES[::-1], SIZES[::-1]):
            rest, at[name] = divmod(rest, size)
        yield index, at


def lines(core_along_y):
    groups = []
    for _, at in places():
        axis = "y4" if at["c"] == core_along_y else "z4"
        if at[axis] == 0:
            groups.append([device(**{**at, axis: k}) for k in range(4)])
    return groups


def exchange(rows, axes, groups=None):
    return lax.all_to_all(rows, axes, split_axis=0, concat_axis=0, axis_index_groups=groups, tiled=True)


def to_place():
    return [
        (index, device(**{**at, "xl": at["z4"] // 2, "yb": at["z4"] % 2, "z4": at["xl"] * 2 + at["yb"]}))
        for index, at in places()
    ]


def body(half_ints, vir_coef, occ_energy, vir_energy):
    xl, y4, yb, c, z4, zb, xh = (lax.axis_index(a) for a in AXES)
    pair = (((xl * 2 + yb) * 2 + xh) * 2 + zb) * 2
    where = jnp.stack([left_orbital(y4, z4, c), pair + c, pair + 1 - c, c])
    keep, give = call(three_index_kernel, [(64, 512)] * 2, [SMEM, VMEM, VMEM])(where, half_ints.reshape(128, 576), vir_coef)
    got = lax.ppermute(give, "c", [(0, 1), (1, 0)])
    to_left, to_right = call(order_kernel, [(128, 512)] * 2, [SMEM, VMEM, VMEM])(where, keep, got)
    right = exchange(to_right.reshape(16, 8, 512), COMPACT)
    (pieces,) = call(first_stage_kernel, [(4, 160, 512)], [VMEM, VMEM])(right.reshape(128, 512), to_left)
    pieces = exchange(pieces, AXES, lines(0))
    (pieces,) = call(second_stage_kernel, [(4, 544, 512)], [VMEM])(pieces)
    own = exchange(pieces, AXES, lines(1))
    other = lax.ppermute(own, "c", [(0, 1), (1, 0)])
    left = jnp.broadcast_to(own[None, :, 512:], (16, 4, 32, 512)).reshape(16, 128, 512)
    left = exchange(left, COMPACT)
    (partial,) = call(
        density_kernel,
        [(16, 128, 512)],
        [SMEM, SMEM, VMEM, VMEM, VMEM, VMEM],
        [pltpu.VMEM((2, 512, 512), jnp.float32), pltpu.VMEM((512, 512), jnp.float32)],
        flops=4 * 512 * 1024 * 2048,
    )(where, occ_energy, left.reshape(16, 16, 8, 512), own, other, vir_energy.reshape(1, 512))
    shares = exchange(partial, COMPACT)
    summed = jnp.sum(shares.astype(jnp.float32), axis=0)
    ordered = summed.reshape(4, 2, 2, 2, 4, 512).transpose(3, 0, 2, 1, 4, 5).reshape(128, 512)
    return lax.ppermute(ordered, AXES, to_place()).reshape(128, 1, 512)


def solution(mesh):
    fine = Mesh(mesh.devices.reshape(SIZES), AXES)
    return jax.shard_map(
        body,
        mesh=fine,
        in_specs=(P(AXES, None, None), P(), P(), P()),
        out_specs=P(("z4", "zb", "xh"), ("xl", "y4", "yb", "c"), None),
        check_vma=False,
    )
```

```python
import jax
import jax.numpy as jnp
from jax import lax
from jax.experimental import pallas as pl
from jax.experimental.pallas import tpu as pltpu
from jax.sharding import Mesh
from jax.sharding import PartitionSpec as P


AXES = ("xl", "y4", "yb", "c", "z4", "zb", "xh")
SIZES = (2, 4, 2, 2, 4, 2, 2)
COMPACT = ("xl", "yb", "xh", "zb")
MIB = 1 << 20
VMEM = pl.BlockSpec(memory_space=pltpu.VMEM)
SMEM = pl.BlockSpec(memory_space=pltpu.SMEM)
ANY = pl.BlockSpec(memory_space=pl.ANY)


def exact_rows(source_row, rows):
    wanted = lax.broadcasted_iota(jnp.int32, source_row.shape, 1)
    selection = (wanted == source_row).astype(jnp.bfloat16)
    return jnp.dot(selection, rows, preferred_element_type=jnp.float32).astype(jnp.bfloat16)


def left_orbital(y4, z4, c):
    return ((z4 // 2) * 8 + y4 * 2 + z4 % 2) * 2 + c


def three_index_kernel(where, half_in, coef_in, keep_ref, give_ref, half_ref, coef_ref, arrived):
    copies = [
        pltpu.make_async_copy(half_in, half_ref, arrived.at[0]),
        pltpu.make_async_copy(coef_in, coef_ref, arrived.at[1]),
    ]
    for copy in copies:
        copy.start()
    for copy in copies:
        copy.wait()
    row = lax.broadcasted_iota(jnp.int32, (128, 128), 0)
    local, pair, pick = row % 4, (row // 4) % 16, row // 64
    ints = jnp.dot(half_ref[...], coef_ref[...], preferred_element_type=jnp.float32).astype(jnp.bfloat16)
    ordered = exact_rows(local * 32 + 2 * pair + (pick + where[3]) % 2, ints)
    keep_ref[...] = ordered[:64]
    give_ref[...] = ordered[64:]


def order_kernel(where, keep_ref, got_ref, left_ref, right_ref):
    core = where[3]
    rows = jnp.concatenate([keep_ref[...], got_ref[...]])
    row = lax.broadcasted_iota(jnp.int32, (128, 128), 0)
    local, first, second = row % 4 + 64 * ((row // 4 + core) % 2), row // 32, (row // 8) % 4
    y4, z4 = jnp.where(core == 0, first, second), jnp.where(core == 0, second, first)
    left_ref[...] = exact_rows(left_orbital(y4, z4, 0) // 2 * 4 + local, rows)
    right_ref[...] = exact_rows(row // 8 * 4 + local, rows)


def first_stage_kernel(right_ref, left_ref, out_ref):
    for target in range(4):
        out_ref[target, 0:128, :] = right_ref[...]
        out_ref[target, 128:160, :] = left_ref[32 * target : 32 * target + 32, :]


def second_stage_kernel(in_ref, out_ref):
    for target in range(4):
        for source in range(4):
            out_ref[target, 128 * source : 128 * source + 128, :] = in_ref[source, 0:128, :]
            at = 128 + 8 * target
            out_ref[target, 512 + 8 * source : 520 + 8 * source, :] = in_ref[source, at : at + 8, :]


def density_kernel(
    where, occ_ref, left_in, own_in, other_in, vir_ref, out_ref, coulomb, total, left_ref, own_ref, other_ref, left_sem, own_sem, other_sem
):
    core = where[3]

    def left_copy(second, first):
        at = second * 4 + first
        return pltpu.make_async_copy(left_in.at[:, at], left_ref.at[second, first], left_sem.at[at])

    def own_copy(second):
        return pltpu.make_async_copy(own_in.at[second, 0:512], own_ref.at[second], own_sem.at[second])

    def other_copy(second):
        at = pl.ds(pl.multiple_of(second * 128, 128), 128)
        return pltpu.make_async_copy(other_in.at[:, at], other_ref.at[second], other_sem.at[second])

    for second in range(4):
        for first in range(4):
            left_copy(second, first).start()
        own_copy(second).start()
        other_copy(second).start()
    down = jnp.broadcast_to(vir_ref[...], (512, 512))
    total[...] = down.T + down
    coulomb[...] = jnp.zeros_like(coulomb)

    def own(second):
        return own_ref[second]

    def other(second):
        return other_ref[second].reshape(512, 512)

    @pl.loop(0, 4)
    def _(second):
        for first in range(4):
            left_copy(second, first).wait()
        own_copy(second).wait()
        other_copy(second).wait()
        left = left_ref[second].reshape(512, 512).T
        coulomb[0] += jnp.dot(left, own(second), preferred_element_type=jnp.float32)
        coulomb[1] += jnp.dot(left, other(second), preferred_element_type=jnp.float32)

    amplitudes = []
    for pick in range(2):
        plain = coulomb[pick]
        flipped = plain.T
        denominator = total[...] - occ_ref[where[0]] - occ_ref[where[1 + pick]]
        amplitudes.append(((2.0 * flipped - plain) / denominator).astype(jnp.bfloat16))

    @pl.loop(0, 4)
    def _(second):
        term = jnp.dot(own(second), amplitudes[0], preferred_element_type=jnp.float32)
        term += jnp.dot(other(second), amplitudes[1], preferred_element_type=jnp.float32)
        term = term.astype(jnp.bfloat16)
        for first in range(4):
            y4, z4 = jnp.where(core == 0, first, second), jnp.where(core == 0, second, first)
            for xl in range(2):
                for yb in range(2):
                    share = xl * 8 + (y4 // 2) * 4 + yb * 2 + y4 % 2
                    at = first * 128 + xl * 64 + yb * 32
                    out_ref[share, pl.ds(pl.multiple_of(z4 * 32, 32), 32), :] = term[at : at + 32]


def sum_kernel(shares, out_ref):
    total = shares[0].astype(jnp.float32)
    for source in range(1, 16):
        total += shares[source].astype(jnp.float32)
    row = lax.broadcasted_iota(jnp.int32, (128, 128), 0)
    local, xh, zb, z4, core = row % 4, (row // 4) % 2, (row // 8) % 2, (row // 16) % 4, row // 64
    source_row = (((z4 * 2 + xh) * 2 + zb) * 2 + core) * 4 + local
    out_ref[...] = exact_rows(source_row, total.astype(jnp.bfloat16))


def call(kernel, shapes, specs, scratch=(), flops=0, vmem=24):
    return pl.pallas_call(
        kernel,
        out_shape=[jax.ShapeDtypeStruct(shape, jnp.bfloat16) for shape in shapes],
        in_specs=specs,
        out_specs=[VMEM] * len(shapes),
        scratch_shapes=list(scratch),
        compiler_params=pltpu.CompilerParams(vmem_limit_bytes=vmem * MIB),
        cost_estimate=pl.CostEstimate(flops=flops, bytes_accessed=2 * MIB, transcendentals=0),
    )


def device(**at):
    index = 0
    for name, size in zip(AXES, SIZES):
        index = index * size + at[name]
    return index


def places():
    for index in range(512):
        at, rest = {}, index
        for name, size in zip(AXES[::-1], SIZES[::-1]):
            rest, at[name] = divmod(rest, size)
        yield index, at


def lines(core_along_y):
    groups = []
    for _, at in places():
        axis = "y4" if at["c"] == core_along_y else "z4"
        if at[axis] == 0:
            groups.append([device(**{**at, axis: k}) for k in range(4)])
    return groups


def exchange(rows, axes, groups=None):
    return lax.all_to_all(rows, axes, split_axis=0, concat_axis=0, axis_index_groups=groups, tiled=True)


def to_place():
    return [
        (index, device(**{**at, "xl": at["z4"] // 2, "yb": at["z4"] % 2, "z4": at["xl"] * 2 + at["yb"]}))
        for index, at in places()
    ]


def body(half_ints, vir_coef, occ_energy, vir_energy):
    xl, y4, yb, c, z4, zb, xh = (lax.axis_index(a) for a in AXES)
    pair = (((xl * 2 + yb) * 2 + xh) * 2 + zb) * 2
    where = jnp.stack([left_orbital(y4, z4, c), pair + c, pair + 1 - c, c])
    keep, give = call(
        three_index_kernel,
        [(64, 512)] * 2,
        [SMEM, ANY, ANY],
        [pltpu.VMEM((128, 576), jnp.bfloat16), pltpu.VMEM((576, 512), jnp.bfloat16), pltpu.SemaphoreType.DMA((2,))],
        vmem=60,
    )(where, half_ints.reshape(128, 576), vir_coef)
    got = lax.ppermute(give, "c", [(0, 1), (1, 0)])
    to_left, to_right = call(order_kernel, [(128, 512)] * 2, [SMEM, VMEM, VMEM])(where, keep, got)
    right = exchange(to_right.reshape(16, 8, 512), COMPACT)
    (pieces,) = call(first_stage_kernel, [(4, 160, 512)], [VMEM, VMEM])(right.reshape(128, 512), to_left)
    pieces = exchange(pieces, AXES, lines(0))
    (pieces,) = call(second_stage_kernel, [(4, 544, 512)], [VMEM], vmem=60)(pieces)
    own = exchange(pieces, AXES, lines(1))
    other = lax.ppermute(own, "c", [(0, 1), (1, 0)])
    left = jnp.broadcast_to(own[None, :, 512:], (16, 4, 32, 512)).reshape(16, 128, 512)
    left = exchange(left, COMPACT)
    (partial,) = call(
        density_kernel,
        [(16, 128, 512)],
        [SMEM, SMEM, ANY, ANY, ANY, VMEM],
        [
            pltpu.VMEM((2, 512, 512), jnp.float32),
            pltpu.VMEM((512, 512), jnp.float32),
            pltpu.VMEM((4, 4, 16, 8, 512), jnp.bfloat16),
            pltpu.VMEM((4, 512, 512), jnp.bfloat16),
            pltpu.VMEM((4, 4, 128, 512), jnp.bfloat16),
            pltpu.SemaphoreType.DMA((16,)),
            pltpu.SemaphoreType.DMA((4,)),
            pltpu.SemaphoreType.DMA((4,)),
        ],
        flops=4 * 512 * 1024 * 2048,
        vmem=56,
    )(where, occ_energy, left.reshape(16, 16, 8, 512), own, other, vir_energy.reshape(1, 512))
    shares = exchange(partial, COMPACT)
    (summed,) = call(sum_kernel, [(128, 512)], [VMEM])(shares)
    placed = lax.ppermute(summed, AXES, to_place())
    return placed.astype(jnp.float32).reshape(128, 1, 512)


def solution(mesh):
    fine = Mesh(mesh.devices.reshape(SIZES), AXES)
    return jax.shard_map(
        body,
        mesh=fine,
        in_specs=(P(AXES, None, None), P(), P(), P()),
        out_specs=P(("z4", "zb", "xh"), ("xl", "y4", "yb", "c"), None),
        check_vma=False,
    )
```

```python
import jax
import jax.numpy as jnp
from jax import lax
from jax.experimental import pallas as pl
from jax.experimental.pallas import tpu as pltpu
from jax.sharding import Mesh
from jax.sharding import PartitionSpec as P


AXES = ("xl", "y4", "yb", "c", "z4", "zb", "xh")
SIZES = (2, 4, 2, 2, 4, 2, 2)
COMPACT = ("xl", "yb", "xh", "zb")
MIB = 1 << 20
VMEM = pl.BlockSpec(memory_space=pltpu.VMEM)
SMEM = pl.BlockSpec(memory_space=pltpu.SMEM)


def exact_rows(source_row, rows):
    wanted = lax.broadcasted_iota(jnp.int32, source_row.shape, 1)
    selection = (wanted == source_row).astype(jnp.bfloat16)
    return jnp.dot(selection, rows, preferred_element_type=jnp.float32).astype(jnp.bfloat16)


def left_orbital(y4, z4, c):
    return ((z4 // 2) * 8 + y4 * 2 + z4 % 2) * 2 + c


def three_index_kernel(where, half_ref, coef_ref, keep_ref, give_ref):
    row = lax.broadcasted_iota(jnp.int32, (128, 128), 0)
    local, pair, pick = row % 4, (row // 4) % 16, row // 64
    ints = jnp.dot(half_ref[...], coef_ref[...], preferred_element_type=jnp.float32).astype(jnp.bfloat16)
    ordered = exact_rows(local * 32 + 2 * pair + (pick + where[3]) % 2, ints)
    keep_ref[...] = ordered[:64]
    give_ref[...] = ordered[64:]


def order_kernel(where, keep_ref, got_ref, left_ref, right_ref):
    core = where[3]
    rows = jnp.concatenate([keep_ref[...], got_ref[...]])
    row = lax.broadcasted_iota(jnp.int32, (128, 128), 0)
    local, first, second = row % 4 + 64 * ((row // 4 + core) % 2), row // 32, (row // 8) % 4
    y4, z4 = jnp.where(core == 0, first, second), jnp.where(core == 0, second, first)
    left_ref[...] = exact_rows(left_orbital(y4, z4, 0) // 2 * 4 + local, rows)
    right_ref[...] = exact_rows(row // 8 * 4 + local, rows)


def first_stage_kernel(right_ref, left_ref, out_ref):
    for target in range(4):
        out_ref[target, 0:128, :] = right_ref[...]
        out_ref[target, 128:160, :] = left_ref[32 * target : 32 * target + 32, :]


def second_stage_kernel(where, in_ref, right_ref, left_ref, own_ref):
    place = where[5]

    def pieces(step):
        at = 128 + 8 * ((place + step) % 4)
        return jnp.concatenate([in_ref[source, pl.ds(pl.multiple_of(at, 8), 8), :] for source in range(4)])

    right_ref[0:32, :] = pieces(2)
    right_ref[544:576, :] = pieces(1)
    left_ref[512:544, :] = pieces(3)
    own_ref[512:544, :] = pieces(0)
    for source in range(4):
        rows = in_ref[source, 0:128, :]
        right_ref[32 + 128 * source : 160 + 128 * source, :] = rows
        left_ref[128 * source : 128 * source + 128, :] = rows
        own_ref[128 * source : 128 * source + 128, :] = rows


def gathered_kernel(own_ref, before_ref, after_ref, opposite_low, opposite_high, right_ref, copies_ref):
    right_ref[0] = own_ref[0:512, :]
    right_ref[1] = after_ref[0:512, :]
    right_ref[2, 0:256, :] = opposite_low[32:288, :]
    right_ref[2, 256:512, :] = opposite_high[...]
    right_ref[3] = before_ref[32:544, :]
    rows = [own_ref[512:544, :], after_ref[512:544, :], opposite_low[0:32, :], before_ref[544:576, :]]
    for copy in range(16):
        for slot in range(4):
            copies_ref[copy, 32 * slot : 32 * slot + 32, :] = rows[slot]


def density_kernel(where, occ_ref, left_ref, own_ref, other_ref, vir_ref, out_ref, coulomb, total):
    core = where[3]
    down = jnp.broadcast_to(vir_ref[...], (512, 512))
    total[...] = down.T + down
    coulomb[...] = jnp.zeros_like(coulomb)

    def own(slot):
        return own_ref[slot]

    def other(slot):
        at = pl.ds(pl.multiple_of((where[5] + slot) % 4 * 128, 128), 128)
        return jnp.concatenate([other_ref[(first + 4 - where[4]) % 4, at, :] for first in range(4)])

    @pl.loop(0, 4)
    def _(slot):
        left = jnp.concatenate([left_ref[:, slot * 4 + first].reshape(128, 512) for first in range(4)]).T
        coulomb[0] += jnp.dot(left, own(slot), preferred_element_type=jnp.float32)
        coulomb[1] += jnp.dot(left, other(slot), preferred_element_type=jnp.float32)

    amplitudes = []
    for pick in range(2):
        plain = coulomb[pick]
        flipped = plain.T
        denominator = total[...] - occ_ref[where[0]] - occ_ref[where[1 + pick]]
        amplitudes.append(((2.0 * flipped - plain) / denominator).astype(jnp.bfloat16))

    @pl.loop(0, 4)
    def _(slot):
        term = jnp.dot(own(slot), amplitudes[0], preferred_element_type=jnp.float32)
        term += jnp.dot(other(slot), amplitudes[1], preferred_element_type=jnp.float32)
        term = term.astype(jnp.bfloat16)
        second = (where[5] + slot) % 4
        for first in range(4):
            y4, z4 = jnp.where(core == 0, first, second), jnp.where(core == 0, second, first)
            for xl in range(2):
                for yb in range(2):
                    share = xl * 8 + (y4 // 2) * 4 + yb * 2 + y4 % 2
                    at = first * 128 + xl * 64 + yb * 32
                    out_ref[share, pl.ds(pl.multiple_of(z4 * 32, 32), 32), :] = term[at : at + 32]


def sum_kernel(shares, out_ref):
    total = shares[0].astype(jnp.float32)
    for source in range(1, 16):
        total += shares[source].astype(jnp.float32)
    row = lax.broadcasted_iota(jnp.int32, (128, 128), 0)
    local, xh, zb, z4, core = row % 4, (row // 4) % 2, (row // 8) % 2, (row // 16) % 4, row // 64
    source_row = (((z4 * 2 + xh) * 2 + zb) * 2 + core) * 4 + local
    out_ref[...] = exact_rows(source_row, total.astype(jnp.bfloat16))


def call(kernel, shapes, specs, scratch=(), flops=0):
    return pl.pallas_call(
        kernel,
        out_shape=[jax.ShapeDtypeStruct(shape, jnp.bfloat16) for shape in shapes],
        in_specs=specs,
        out_specs=[VMEM] * len(shapes),
        scratch_shapes=list(scratch),
        compiler_params=pltpu.CompilerParams(vmem_limit_bytes=24 * MIB),
        cost_estimate=pl.CostEstimate(flops=flops, bytes_accessed=2 * MIB, transcendentals=0),
    )


def device(**at):
    index = 0
    for name, size in zip(AXES, SIZES):
        index = index * size + at[name]
    return index


def places():
    for index in range(512):
        at, rest = {}, index
        for name, size in zip(AXES[::-1], SIZES[::-1]):
            rest, at[name] = divmod(rest, size)
        yield index, at


def first_lines():
    groups = []
    for _, at in places():
        axis = "z4" if at["c"] else "y4"
        if at[axis] == 0:
            groups.append([device(**{**at, axis: k}) for k in range(4)])
    return groups


def along_line(step):
    pairs = []
    for index, at in places():
        axis = "y4" if at["c"] else "z4"
        pairs.append((index, device(**{**at, axis: (at[axis] + step) % 4})))
    return pairs


def exchange(rows, axes, groups=None):
    return lax.all_to_all(rows, axes, split_axis=0, concat_axis=0, axis_index_groups=groups, tiled=True)


def to_place():
    return [
        (index, device(**{**at, "xl": at["z4"] // 2, "yb": at["z4"] % 2, "z4": at["xl"] * 2 + at["yb"]}))
        for index, at in places()
    ]


def body(half_ints, vir_coef, occ_energy, vir_energy):
    xl, y4, yb, c, z4, zb, xh = (lax.axis_index(a) for a in AXES)
    pair = (((xl * 2 + yb) * 2 + xh) * 2 + zb) * 2
    first, second = jnp.where(c == 0, y4, z4), jnp.where(c == 0, z4, y4)
    where = jnp.stack([left_orbital(y4, z4, c), pair + c, pair + 1 - c, c, first, second])
    keep, give = call(three_index_kernel, [(64, 512)] * 2, [SMEM, VMEM, VMEM])(where, half_ints.reshape(128, 576), vir_coef)
    got = lax.ppermute(give, "c", [(0, 1), (1, 0)])
    to_left, to_right = call(order_kernel, [(128, 512)] * 2, [SMEM, VMEM, VMEM])(where, keep, got)
    right = exchange(to_right.reshape(16, 8, 512), COMPACT)
    (pieces,) = call(first_stage_kernel, [(4, 160, 512)], [VMEM, VMEM])(right.reshape(128, 512), to_left)
    pieces = exchange(pieces, AXES, first_lines())
    to_next, to_last, own = call(second_stage_kernel, [(576, 512), (544, 512), (544, 512)], [SMEM, VMEM])(where, pieces)
    before = lax.ppermute(to_next, AXES, along_line(1))
    after = lax.ppermute(to_last, AXES, along_line(-1))
    opposite_low = lax.ppermute(before[:288], AXES, along_line(1))
    opposite_high = lax.ppermute(after[256:512], AXES, along_line(-1))
    own, copies = call(gathered_kernel, [(4, 512, 512), (16, 128, 512)], [VMEM] * 5)(
        own, before, after, opposite_low, opposite_high
    )
    other = lax.ppermute(own, "c", [(0, 1), (1, 0)])
    left = exchange(copies, COMPACT)
    (partial,) = call(
        density_kernel,
        [(16, 128, 512)],
        [SMEM, SMEM, VMEM, VMEM, VMEM, VMEM],
        [pltpu.VMEM((2, 512, 512), jnp.float32), pltpu.VMEM((512, 512), jnp.float32)],
        flops=4 * 512 * 1024 * 2048,
    )(where, occ_energy, left.reshape(16, 16, 8, 512), own, other, vir_energy.reshape(1, 512))
    shares = exchange(partial, COMPACT)
    (summed,) = call(sum_kernel, [(128, 512)], [VMEM])(shares)
    placed = lax.ppermute(summed, AXES, to_place())
    return placed.astype(jnp.float32).reshape(128, 1, 512)


def solution(mesh):
    fine = Mesh(mesh.devices.reshape(SIZES), AXES)
    return jax.shard_map(
        body,
        mesh=fine,
        in_specs=(P(AXES, None, None), P(), P(), P()),
        out_specs=P(("z4", "zb", "xh"), ("xl", "y4", "yb", "c"), None),
        check_vma=False,
    )
```

```python
import jax
import jax.numpy as jnp
from jax import lax
from jax.experimental import pallas as pl
from jax.experimental.pallas import tpu as pltpu
from jax.sharding import Mesh
from jax.sharding import PartitionSpec as P


AXES = ("xl", "y4", "yb", "c", "z4", "zb", "xh")
SIZES = (2, 4, 2, 2, 4, 2, 2)
COMPACT = ("xl", "yb", "xh", "zb")
MIB = 1 << 20
VMEM = pl.BlockSpec(memory_space=pltpu.VMEM)
SMEM = pl.BlockSpec(memory_space=pltpu.SMEM)


def exact_rows(source_row, rows):
    wanted = lax.broadcasted_iota(jnp.int32, source_row.shape, 1)
    selection = (wanted == source_row).astype(jnp.bfloat16)
    return jnp.dot(selection, rows, preferred_element_type=jnp.float32).astype(jnp.bfloat16)


def left_orbital(y4, z4, c):
    return ((z4 // 2) * 8 + y4 * 2 + z4 % 2) * 2 + c


def three_index_kernel(where, half_ref, coef_ref, keep_ref, give_ref):
    row = lax.broadcasted_iota(jnp.int32, (128, 128), 0)
    local, pair, pick = row % 4, (row // 4) % 16, row // 64
    ints = jnp.dot(half_ref[...], coef_ref[...], preferred_element_type=jnp.float32).astype(jnp.bfloat16)
    ordered = exact_rows(local * 32 + 2 * pair + (pick + where[3]) % 2, ints)
    keep_ref[...] = ordered[:64]
    give_ref[...] = ordered[64:]


def order_kernel(where, keep_ref, got_ref, left_ref, right_ref):
    rows = jnp.concatenate([keep_ref[...], got_ref[...]])
    row = lax.broadcasted_iota(jnp.int32, (128, 128), 0)
    local = row % 4 + 64 * ((row // 4 + where[3]) % 2)
    left_ref[...] = exact_rows(left_orbital(row // 32, (row // 8) % 4, 0) // 2 * 4 + local, rows)
    right_ref[...] = exact_rows(row // 8 * 4 + local, rows)


def gather(own_ref, before_ref, after_ref, low_ref, high_ref, out_ref):
    out_ref[0] = own_ref[...]
    out_ref[1] = after_ref[...]
    out_ref[2, 0:256, :] = low_ref[...]
    out_ref[2, 256:512, :] = high_ref[...]
    out_ref[3] = before_ref[...]


def density_kernel(where, occ_ref, vir_ref, left_ref, *refs):
    *pieces, out_ref, coulomb, total, own_ref, other_ref = refs
    core = where[3]
    gather(*pieces[:5], own_ref)
    gather(*pieces[5:], other_ref)
    down = jnp.broadcast_to(vir_ref[...], (512, 512))
    total[...] = down.T + down
    coulomb[...] = jnp.zeros_like(coulomb)

    def own(slot):
        return own_ref[slot]

    def other(slot):
        at = pl.ds(pl.multiple_of((where[5] + slot) % 4 * 128, 128), 128)
        return jnp.concatenate([other_ref[(first + 4 - where[4]) % 4, at, :] for first in range(4)])

    @pl.loop(0, 4)
    def _(slot):
        second = (where[5] + slot) % 4
        at = [jnp.where(core == 0, first * 4 + second, second * 4 + first) for first in range(4)]
        left = jnp.concatenate([left_ref[:, k].reshape(128, 512) for k in at]).T
        coulomb[0] += jnp.dot(left, own(slot), preferred_element_type=jnp.float32)
        coulomb[1] += jnp.dot(left, other(slot), preferred_element_type=jnp.float32)

    amplitudes = []
    for pick in range(2):
        plain = coulomb[pick]
        flipped = plain.T
        denominator = total[...] - occ_ref[where[0]] - occ_ref[where[1 + pick]]
        amplitudes.append(((2.0 * flipped - plain) / denominator).astype(jnp.bfloat16))

    @pl.loop(0, 4)
    def _(slot):
        term = jnp.dot(own(slot), amplitudes[0], preferred_element_type=jnp.float32)
        term += jnp.dot(other(slot), amplitudes[1], preferred_element_type=jnp.float32)
        term = term.astype(jnp.bfloat16)
        second = (where[5] + slot) % 4
        for first in range(4):
            y4, z4 = jnp.where(core == 0, first, second), jnp.where(core == 0, second, first)
            for xl in range(2):
                for yb in range(2):
                    share = xl * 8 + (y4 // 2) * 4 + yb * 2 + y4 % 2
                    at = first * 128 + xl * 64 + yb * 32
                    out_ref[share, pl.ds(pl.multiple_of(z4 * 32, 32), 32), :] = term[at : at + 32]


def sum_kernel(shares, out_ref):
    total = shares[0].astype(jnp.float32)
    for source in range(1, 16):
        total += shares[source].astype(jnp.float32)
    row = lax.broadcasted_iota(jnp.int32, (128, 128), 0)
    local, xh, zb, z4, core = row % 4, (row // 4) % 2, (row // 8) % 2, (row // 16) % 4, row // 64
    source_row = (((z4 * 2 + xh) * 2 + zb) * 2 + core) * 4 + local
    out_ref[...] = exact_rows(source_row, total.astype(jnp.bfloat16))


def call(kernel, shapes, specs, scratch=(), flops=0):
    return pl.pallas_call(
        kernel,
        out_shape=[jax.ShapeDtypeStruct(shape, jnp.bfloat16) for shape in shapes],
        in_specs=specs,
        out_specs=[VMEM] * len(shapes),
        scratch_shapes=list(scratch),
        compiler_params=pltpu.CompilerParams(vmem_limit_bytes=24 * MIB),
        cost_estimate=pl.CostEstimate(flops=flops, bytes_accessed=2 * MIB, transcendentals=0),
    )


def device(**at):
    index = 0
    for name, size in zip(AXES, SIZES):
        index = index * size + at[name]
    return index


def places():
    for index in range(512):
        at, rest = {}, index
        for name, size in zip(AXES[::-1], SIZES[::-1]):
            rest, at[name] = divmod(rest, size)
        yield index, at


def first_lines():
    groups = []
    for _, at in places():
        axis = "z4" if at["c"] else "y4"
        if at[axis] == 0:
            groups.append([device(**{**at, axis: k}) for k in range(4)])
    return groups


def along_line(step):
    pairs = []
    for index, at in places():
        axis = "y4" if at["c"] else "z4"
        pairs.append((index, device(**{**at, axis: (at[axis] + step) % 4})))
    return pairs


def exchange(rows, axes, groups=None):
    return lax.all_to_all(rows, axes, split_axis=0, concat_axis=0, axis_index_groups=groups, tiled=True)


def to_place():
    return [
        (index, device(**{**at, "xl": at["z4"] // 2, "yb": at["z4"] % 2, "z4": at["xl"] * 2 + at["yb"]}))
        for index, at in places()
    ]


def body(half_ints, vir_coef, occ_energy, vir_energy):
    xl, y4, yb, c, z4, zb, xh = (lax.axis_index(a) for a in AXES)
    pair = (((xl * 2 + yb) * 2 + xh) * 2 + zb) * 2
    first, second = jnp.where(c == 0, y4, z4), jnp.where(c == 0, z4, y4)
    where = jnp.stack([left_orbital(y4, z4, c), pair + c, pair + 1 - c, c, first, second])
    keep, give = call(three_index_kernel, [(64, 512)] * 2, [SMEM, VMEM, VMEM])(where, half_ints.reshape(128, 576), vir_coef)
    got = lax.ppermute(give, "c", [(0, 1), (1, 0)])
    to_left, to_right = call(order_kernel, [(128, 512)] * 2, [SMEM, VMEM, VMEM])(where, keep, got)
    right = exchange(to_right.reshape(16, 8, 512), COMPACT).reshape(128, 512)
    shard = exchange(to_left.reshape(16, 8, 512), ("y4", "z4")).reshape(128, 512)
    line = exchange(jnp.broadcast_to(right[None], (4, 128, 512)), AXES, first_lines()).reshape(512, 512)
    before = lax.ppermute(line, AXES, along_line(1))
    after = lax.ppermute(line, AXES, along_line(-1))
    left = exchange(jnp.broadcast_to(shard[None], (16, 128, 512)), COMPACT)
    pieces = [
        line,
        before,
        after,
        lax.ppermute(before[:256], AXES, along_line(1)),
        lax.ppermute(after[256:], AXES, along_line(-1)),
    ]
    others = [lax.ppermute(piece, "c", [(0, 1), (1, 0)]) for piece in pieces]
    (partial,) = call(
        density_kernel,
        [(16, 128, 512)],
        [SMEM, SMEM] + [VMEM] * 12,
        [
            pltpu.VMEM((2, 512, 512), jnp.float32),
            pltpu.VMEM((512, 512), jnp.float32),
            pltpu.VMEM((4, 512, 512), jnp.bfloat16),
            pltpu.VMEM((4, 512, 512), jnp.bfloat16),
        ],
        flops=4 * 512 * 1024 * 2048,
    )(where, occ_energy, vir_energy.reshape(1, 512), left.reshape(16, 16, 8, 512), *pieces, *others)
    shares = exchange(partial, COMPACT)
    (summed,) = call(sum_kernel, [(128, 512)], [VMEM])(shares)
    placed = lax.ppermute(summed, AXES, to_place())
    return placed.astype(jnp.float32).reshape(128, 1, 512)


def solution(mesh):
    fine = Mesh(mesh.devices.reshape(SIZES), AXES)
    return jax.shard_map(
        body,
        mesh=fine,
        in_specs=(P(AXES, None, None), P(), P(), P()),
        out_specs=P(("z4", "zb", "xh"), ("xl", "y4", "yb", "c"), None),
        check_vma=False,
    )
```

```python
import jax
import jax.numpy as jnp
from jax import lax
from jax.experimental import pallas as pl
from jax.experimental.pallas import tpu as pltpu
from jax.sharding import Mesh
from jax.sharding import PartitionSpec as P


AXES = ("xl", "y4", "yb", "c", "z4", "zb", "xh")
SIZES = (2, 4, 2, 2, 4, 2, 2)
COMPACT = ("xl", "yb", "xh", "zb")
MIB = 1 << 20
VMEM = pl.BlockSpec(memory_space=pltpu.VMEM)
SMEM = pl.BlockSpec(memory_space=pltpu.SMEM)


def exact_rows(source_row, rows):
    wanted = lax.broadcasted_iota(jnp.int32, source_row.shape, 1)
    selection = (wanted == source_row).astype(jnp.bfloat16)
    return jnp.dot(selection, rows, preferred_element_type=jnp.float32).astype(jnp.bfloat16)


def left_orbital(y4, z4, c):
    return ((z4 // 2) * 8 + y4 * 2 + z4 % 2) * 2 + c


def three_index_kernel(where, half_ref, coef_ref, keep_ref, give_ref):
    row = lax.broadcasted_iota(jnp.int32, (128, 128), 0)
    local, pair, pick = row % 4, (row // 4) % 16, row // 64
    ints = jnp.dot(half_ref[...], coef_ref[...], preferred_element_type=jnp.float32).astype(jnp.bfloat16)
    ordered = exact_rows(local * 32 + 2 * pair + (pick + where[3]) % 2, ints)
    keep_ref[...] = ordered[:64]
    give_ref[...] = ordered[64:]


def order_kernel(where, keep_ref, got_ref, left_ref, right_ref):
    core = where[3]
    rows = jnp.concatenate([keep_ref[...], got_ref[...]])
    row = lax.broadcasted_iota(jnp.int32, (128, 128), 0)
    local, first, second = row % 4 + 64 * ((row // 4 + core) % 2), row // 32, (row // 8) % 4
    y4, z4 = jnp.where(core == 0, first, second), jnp.where(core == 0, second, first)
    left_ref[...] = exact_rows(left_orbital(y4, z4, 0) // 2 * 4 + local, rows)
    right_ref[...] = exact_rows(row // 8 * 4 + local, rows)


def first_stage_kernel(right_ref, left_ref, out_ref):
    for target in range(4):
        out_ref[target, 0:128, :] = right_ref[...]
        out_ref[target, 128:160, :] = left_ref[32 * target : 32 * target + 32, :]


def second_stage_kernel(in_ref, out_ref):
    for target in range(4):
        for source in range(4):
            out_ref[target, 128 * source : 128 * source + 128, :] = in_ref[source, 0:128, :]
            at = 128 + 8 * target
            out_ref[target, 512 + 8 * source : 520 + 8 * source, :] = in_ref[source, at : at + 8, :]


def density_kernel(where, occ_ref, left_ref, own_ref, other_ref, vir_ref, out_ref, coulomb, total):
    core = where[3]
    down = jnp.broadcast_to(vir_ref[...], (512, 512))
    total[...] = down.T + down
    coulomb[...] = jnp.zeros_like(coulomb)

    def own(second):
        return own_ref[second, 0:512, :]

    def other(second):
        at = pl.ds(pl.multiple_of(second * 128, 128), 128)
        return jnp.concatenate([other_ref[first, at, :] for first in range(4)])

    @pl.loop(0, 4)
    def _(second):
        left = jnp.concatenate([left_ref[:, second * 4 + first].reshape(128, 512) for first in range(4)]).T
        coulomb[0] += jnp.dot(left, own(second), preferred_element_type=jnp.float32)
        coulomb[1] += jnp.dot(left, other(second), preferred_element_type=jnp.float32)

    amplitudes = []
    for pick in range(2):
        plain = coulomb[pick]
        flipped = plain.T
        denominator = total[...] - occ_ref[where[0]] - occ_ref[where[1 + pick]]
        amplitudes.append(((2.0 * flipped - plain) / denominator).astype(jnp.bfloat16))

    @pl.loop(0, 4)
    def _(second):
        term = jnp.dot(own(second), amplitudes[0], preferred_element_type=jnp.float32)
        term += jnp.dot(other(second), amplitudes[1], preferred_element_type=jnp.float32)
        term = term.astype(jnp.bfloat16)
        for first in range(4):
            y4, z4 = jnp.where(core == 0, first, second), jnp.where(core == 0, second, first)
            for xl in range(2):
                for yb in range(2):
                    share = xl * 8 + (y4 // 2) * 4 + yb * 2 + y4 % 2
                    at = first * 128 + xl * 64 + yb * 32
                    out_ref[share, pl.ds(pl.multiple_of(z4 * 32, 32), 32), :] = term[at : at + 32]


def sum_kernel(shares, out_ref):
    total = shares[0].astype(jnp.float32)
    for source in range(1, 16):
        total += shares[source].astype(jnp.float32)
    row = lax.broadcasted_iota(jnp.int32, (128, 128), 0)
    local, xh, zb, z4, core = row % 4, (row // 4) % 2, (row // 8) % 2, (row // 16) % 4, row // 64
    source_row = (((z4 * 2 + xh) * 2 + zb) * 2 + core) * 4 + local
    out_ref[...] = exact_rows(source_row, total.astype(jnp.bfloat16))


def call(kernel, shapes, specs, scratch=(), flops=0):
    return pl.pallas_call(
        kernel,
        out_shape=[jax.ShapeDtypeStruct(shape, jnp.bfloat16) for shape in shapes],
        in_specs=specs,
        out_specs=[VMEM] * len(shapes),
        scratch_shapes=list(scratch),
        compiler_params=pltpu.CompilerParams(vmem_limit_bytes=24 * MIB),
        cost_estimate=pl.CostEstimate(flops=flops, bytes_accessed=2 * MIB, transcendentals=0),
    )


def device(**at):
    index = 0
    for name, size in zip(AXES, SIZES):
        index = index * size + at[name]
    return index


def places():
    for index in range(512):
        at, rest = {}, index
        for name, size in zip(AXES[::-1], SIZES[::-1]):
            rest, at[name] = divmod(rest, size)
        yield index, at


def lines(core_along_y):
    groups = []
    for _, at in places():
        axis = "y4" if at["c"] == core_along_y else "z4"
        if at[axis] == 0:
            groups.append([device(**{**at, axis: k}) for k in range(4)])
    return groups


def exchange(rows, axes, groups=None):
    return lax.all_to_all(rows, axes, split_axis=0, concat_axis=0, axis_index_groups=groups, tiled=True)


def to_place():
    return [
        (index, device(**{**at, "xl": at["z4"] // 2, "yb": at["z4"] % 2, "z4": at["xl"] * 2 + at["yb"]}))
        for index, at in places()
    ]


def body(half_ints, vir_coef, occ_energy, vir_energy):
    xl, y4, yb, c, z4, zb, xh = (lax.axis_index(a) for a in AXES)
    pair = (((xl * 2 + yb) * 2 + xh) * 2 + zb) * 2
    where = jnp.stack([left_orbital(y4, z4, c), pair + c, pair + 1 - c, c])
    keep, give = call(three_index_kernel, [(64, 512)] * 2, [SMEM, VMEM, VMEM])(where, half_ints.reshape(128, 576), vir_coef)
    got = lax.ppermute(give, "c", [(0, 1), (1, 0)])
    to_left, to_right = call(order_kernel, [(128, 512)] * 2, [SMEM, VMEM, VMEM])(where, keep, got)
    right = exchange(to_right.reshape(16, 8, 512), COMPACT)
    (pieces,) = call(first_stage_kernel, [(4, 160, 512)], [VMEM, VMEM])(right.reshape(128, 512), to_left)
    pieces = exchange(pieces, AXES, lines(0))
    (pieces,) = call(second_stage_kernel, [(4, 544, 512)], [VMEM])(pieces)
    own = exchange(pieces, AXES, lines(1))
    other = lax.ppermute(own, "c", [(0, 1), (1, 0)])
    left = jnp.broadcast_to(own[None, :, 512:], (16, 4, 32, 512)).reshape(16, 128, 512)
    left = exchange(left, COMPACT)
    (partial,) = call(
        density_kernel,
        [(16, 128, 512)],
        [SMEM, SMEM, VMEM, VMEM, VMEM, VMEM],
        [pltpu.VMEM((2, 512, 512), jnp.float32), pltpu.VMEM((512, 512), jnp.float32)],
        flops=4 * 512 * 1024 * 2048,
    )(where, occ_energy, left.reshape(16, 16, 8, 512), own, other, vir_energy.reshape(1, 512))
    shares = exchange(partial, COMPACT)
    (summed,) = call(sum_kernel, [(128, 512)], [VMEM])(shares)
    placed = lax.ppermute(summed, AXES, to_place())
    return placed.astype(jnp.float32).reshape(128, 1, 512)


def solution(mesh):
    fine = Mesh(mesh.devices.reshape(SIZES), AXES)
    return jax.shard_map(
        body,
        mesh=fine,
        in_specs=(P(AXES, None, None), P(), P(), P()),
        out_specs=P(("z4", "zb", "xh"), ("xl", "y4", "yb", "c"), None),
        check_vma=False,
    )
```

```python
import jax
import jax.numpy as jnp
from jax import lax
from jax.experimental import pallas as pl
from jax.experimental.pallas import tpu as pltpu
from jax.sharding import Mesh
from jax.sharding import PartitionSpec as P


AXES = ("xl", "y4", "yb", "c", "z4", "zb", "xh")
SIZES = (2, 4, 2, 2, 4, 2, 2)
COMPACT = ("xl", "yb", "xh", "zb")
MIB = 1 << 20
VMEM = pl.BlockSpec(memory_space=pltpu.VMEM)
SMEM = pl.BlockSpec(memory_space=pltpu.SMEM)


def exact_rows(source_row, rows):
    wanted = lax.broadcasted_iota(jnp.int32, source_row.shape, 1)
    selection = (wanted == source_row).astype(jnp.bfloat16)
    return jnp.dot(selection, rows, preferred_element_type=jnp.float32).astype(jnp.bfloat16)


def left_orbital(y4, z4, c):
    return ((z4 // 2) * 8 + y4 * 2 + z4 % 2) * 2 + c


def three_index_kernel(where, half_ref, coef_ref, keep_ref, give_ref):
    row = lax.broadcasted_iota(jnp.int32, (128, 128), 0)
    local, pair, pick = row % 4, (row // 4) % 16, row // 64
    ints = jnp.dot(half_ref[...], coef_ref[...], preferred_element_type=jnp.float32).astype(jnp.bfloat16)
    ordered = exact_rows(local * 32 + 2 * pair + (pick + where[3]) % 2, ints)
    keep_ref[...] = ordered[:64]
    give_ref[...] = ordered[64:]


def order_kernel(where, keep_ref, got_ref, left_ref, right_ref):
    core = where[3]
    rows = jnp.concatenate([keep_ref[...], got_ref[...]])
    row = lax.broadcasted_iota(jnp.int32, (128, 128), 0)
    local, first, second = row % 4 + 64 * ((row // 4 + core) % 2), row // 32, (row // 8) % 4
    y4, z4 = jnp.where(core == 0, first, second), jnp.where(core == 0, second, first)
    left_ref[...] = exact_rows(left_orbital(y4, z4, 0) // 2 * 4 + local, rows)
    right_ref[...] = exact_rows(row // 8 * 4 + local, rows)


def first_stage_kernel(right_ref, left_ref, out_ref):
    for target in range(4):
        out_ref[target, 0:128, :] = right_ref[...]
        out_ref[target, 128:160, :] = left_ref[32 * target : 32 * target + 32, :]


def second_stage_kernel(where, in_ref, out_ref, keep_ref):
    place = where[5]

    def pieces(step):
        at = pl.ds(pl.multiple_of(128 + 8 * (place ^ step), 8), 8)
        return jnp.concatenate([in_ref[source, at, :] for source in range(4)])

    for source in range(4):
        out_ref[128 * source : 128 * source + 128, :] = in_ref[source, 0:128, :]
    out_ref[512:544, :] = pieces(1)
    out_ref[544:576, :] = pieces(2)
    keep_ref[0:32, :] = pieces(0)
    keep_ref[32:64, :] = pieces(3)


def third_stage_kernel(own_ref, near_ref, keep_ref, out_ref):
    out_ref[0:512, :] = own_ref[0:512, :]
    out_ref[512:1024, :] = near_ref[0:512, :]
    out_ref[1024:1056, :] = keep_ref[32:64, :]
    out_ref[1056:1088, :] = near_ref[544:576, :]


def shard_kernel(keep_ref, near_ref, far_ref, out_ref):
    out_ref[0:32, :] = keep_ref[0:32, :]
    out_ref[32:64, :] = near_ref[512:544, :]
    out_ref[64:96, :] = far_ref[1056:1088, :]
    out_ref[96:128, :] = far_ref[1024:1056, :]


def gather(near_ref, far_ref, out_ref):
    out_ref[0] = near_ref[0:512, :]
    out_ref[1] = near_ref[512:1024, :]
    out_ref[2] = far_ref[512:1024, :]
    out_ref[3] = far_ref[0:512, :]


def density_kernel(where, occ_ref, vir_ref, left_ref, *refs):
    *halves, out_ref, coulomb, total, own_ref, other_ref = refs
    core = where[3]
    gather(*halves[:2], own_ref)
    gather(*halves[2:], other_ref)
    down = jnp.broadcast_to(vir_ref[...], (512, 512))
    total[...] = down.T + down
    coulomb[...] = jnp.zeros_like(coulomb)

    def own(slot):
        return own_ref[slot]

    def other(slot):
        at = pl.ds(pl.multiple_of((where[5] ^ slot) * 128, 128), 128)
        return jnp.concatenate([other_ref[where[4] ^ first, at, :] for first in range(4)])

    @pl.loop(0, 4)
    def _(slot):
        left = jnp.concatenate([left_ref[:, slot * 4 + first].reshape(128, 512) for first in range(4)]).T
        coulomb[0] += jnp.dot(left, own(slot), preferred_element_type=jnp.float32)
        coulomb[1] += jnp.dot(left, other(slot), preferred_element_type=jnp.float32)

    amplitudes = []
    for pick in range(2):
        plain = coulomb[pick]
        flipped = plain.T
        denominator = total[...] - occ_ref[where[0]] - occ_ref[where[1 + pick]]
        amplitudes.append(((2.0 * flipped - plain) / denominator).astype(jnp.bfloat16))

    @pl.loop(0, 4)
    def _(slot):
        term = jnp.dot(own(slot), amplitudes[0], preferred_element_type=jnp.float32)
        term += jnp.dot(other(slot), amplitudes[1], preferred_element_type=jnp.float32)
        term = term.astype(jnp.bfloat16)
        second = where[5] ^ slot
        for first in range(4):
            y4, z4 = jnp.where(core == 0, first, second), jnp.where(core == 0, second, first)
            for xl in range(2):
                for yb in range(2):
                    share = xl * 8 + (y4 // 2) * 4 + yb * 2 + y4 % 2
                    at = first * 128 + xl * 64 + yb * 32
                    out_ref[share, pl.ds(pl.multiple_of(z4 * 32, 32), 32), :] = term[at : at + 32]


def sum_kernel(shares, out_ref):
    total = shares[0].astype(jnp.float32)
    for source in range(1, 16):
        total += shares[source].astype(jnp.float32)
    row = lax.broadcasted_iota(jnp.int32, (128, 128), 0)
    local, xh, zb, z4, core = row % 4, (row // 4) % 2, (row // 8) % 2, (row // 16) % 4, row // 64
    source_row = (((z4 * 2 + xh) * 2 + zb) * 2 + core) * 4 + local
    out_ref[...] = exact_rows(source_row, total.astype(jnp.bfloat16))


def call(kernel, shapes, specs, scratch=(), flops=0):
    return pl.pallas_call(
        kernel,
        out_shape=[jax.ShapeDtypeStruct(shape, jnp.bfloat16) for shape in shapes],
        in_specs=specs,
        out_specs=[VMEM] * len(shapes),
        scratch_shapes=list(scratch),
        compiler_params=pltpu.CompilerParams(vmem_limit_bytes=24 * MIB),
        cost_estimate=pl.CostEstimate(flops=flops, bytes_accessed=2 * MIB, transcendentals=0),
    )


def device(**at):
    index = 0
    for name, size in zip(AXES, SIZES):
        index = index * size + at[name]
    return index


def places():
    for index in range(512):
        at, rest = {}, index
        for name, size in zip(AXES[::-1], SIZES[::-1]):
            rest, at[name] = divmod(rest, size)
        yield index, at


def first_lines():
    groups = []
    for _, at in places():
        axis = "z4" if at["c"] else "y4"
        if at[axis] == 0:
            groups.append([device(**{**at, axis: k}) for k in range(4)])
    return groups


def along_line(step):
    pairs = []
    for index, at in places():
        axis = "y4" if at["c"] else "z4"
        pairs.append((index, device(**{**at, axis: at[axis] ^ step})))
    return pairs


def exchange(rows, axes, groups=None):
    return lax.all_to_all(rows, axes, split_axis=0, concat_axis=0, axis_index_groups=groups, tiled=True)


def to_place():
    return [
        (index, device(**{**at, "xl": at["z4"] // 2, "yb": at["z4"] % 2, "z4": at["xl"] * 2 + at["yb"]}))
        for index, at in places()
    ]


def body(half_ints, vir_coef, occ_energy, vir_energy):
    xl, y4, yb, c, z4, zb, xh = (lax.axis_index(a) for a in AXES)
    pair = (((xl * 2 + yb) * 2 + xh) * 2 + zb) * 2
    first, second = jnp.where(c == 0, y4, z4), jnp.where(c == 0, z4, y4)
    where = jnp.stack([left_orbital(y4, z4, c), pair + c, pair + 1 - c, c, first, second])
    keep, give = call(three_index_kernel, [(64, 512)] * 2, [SMEM, VMEM, VMEM])(where, half_ints.reshape(128, 576), vir_coef)
    got = lax.ppermute(give, "c", [(0, 1), (1, 0)])
    to_left, to_right = call(order_kernel, [(128, 512)] * 2, [SMEM, VMEM, VMEM])(where, keep, got)
    right = exchange(to_right.reshape(16, 8, 512), COMPACT)
    (pieces,) = call(first_stage_kernel, [(4, 160, 512)], [VMEM, VMEM])(right.reshape(128, 512), to_left)
    pieces = exchange(pieces, AXES, first_lines())
    to_near, keep = call(second_stage_kernel, [(576, 512), (64, 512)], [SMEM, VMEM])(where, pieces)
    near = lax.ppermute(to_near, AXES, along_line(1))
    (half,) = call(third_stage_kernel, [(1088, 512)], [VMEM] * 3)(to_near, near, keep)
    far = lax.ppermute(half, AXES, along_line(3))
    (shard,) = call(shard_kernel, [(128, 512)], [VMEM] * 3)(keep, near, far)
    left = exchange(jnp.broadcast_to(shard[None], (16, 128, 512)), COMPACT)
    halves = [half, far, *(lax.ppermute(rows, "c", [(0, 1), (1, 0)]) for rows in (half, far))]
    (partial,) = call(
        density_kernel,
        [(16, 128, 512)],
        [SMEM, SMEM] + [VMEM] * 6,
        [
            pltpu.VMEM((2, 512, 512), jnp.float32),
            pltpu.VMEM((512, 512), jnp.float32),
            pltpu.VMEM((4, 512, 512), jnp.bfloat16),
            pltpu.VMEM((4, 512, 512), jnp.bfloat16),
        ],
        flops=4 * 512 * 1024 * 2048,
    )(where, occ_energy, vir_energy.reshape(1, 512), left.reshape(16, 16, 8, 512), *halves)
    shares = exchange(partial, COMPACT)
    (summed,) = call(sum_kernel, [(128, 512)], [VMEM])(shares)
    placed = lax.ppermute(summed, AXES, to_place())
    return placed.astype(jnp.float32).reshape(128, 1, 512)


def solution(mesh):
    fine = Mesh(mesh.devices.reshape(SIZES), AXES)
    return jax.shard_map(
        body,
        mesh=fine,
        in_specs=(P(AXES, None, None), P(), P(), P()),
        out_specs=P(("z4", "zb", "xh"), ("xl", "y4", "yb", "c"), None),
        check_vma=False,
    )
```

```python
import jax
import jax.numpy as jnp
from jax import lax
from jax.experimental import pallas as pl
from jax.experimental.pallas import tpu as pltpu
from jax.sharding import Mesh
from jax.sharding import PartitionSpec as P


AXES = ("xl", "y4", "yb", "c", "z4", "zb", "xh")
SIZES = (2, 4, 2, 2, 4, 2, 2)
COMPACT = ("xl", "yb", "xh", "zb")
MIB = 1 << 20
VMEM = pl.BlockSpec(memory_space=pltpu.VMEM)
SMEM = pl.BlockSpec(memory_space=pltpu.SMEM)


def exact_rows(source_row, rows):
    wanted = lax.broadcasted_iota(jnp.int32, source_row.shape, 1)
    selection = (wanted == source_row).astype(jnp.bfloat16)
    return jnp.dot(selection, rows, preferred_element_type=jnp.float32).astype(jnp.bfloat16)


def left_orbital(y4, z4, c):
    return ((z4 // 2) * 8 + y4 * 2 + z4 % 2) * 2 + c


def kept_rows(core, half_ref, coef_ref):
    row = lax.broadcasted_iota(jnp.int32, (64, 128), 0)
    half_ints = exact_rows(row % 4 * 32 + row // 4 * 2 + core, half_ref[...])
    return jnp.dot(half_ints, coef_ref[...], preferred_element_type=jnp.float32).astype(jnp.bfloat16)


def own_rows_kernel(where, half_ref, coef_ref, out_ref):
    out_ref[...] = kept_rows(where[3], half_ref, coef_ref)


def three_index_kernel(where, own_ref, got_ref, coef_ref, left_ref, right_ref):
    core = where[3]
    rows = jnp.concatenate([own_ref[...], kept_rows(core, got_ref, coef_ref)])
    row = lax.broadcasted_iota(jnp.int32, (128, 128), 0)
    local, first, second = row % 4 + 64 * ((row // 4 + core) % 2), row // 32, (row // 8) % 4
    y4, z4 = jnp.where(core == 0, first, second), jnp.where(core == 0, second, first)
    left_ref[...] = exact_rows(left_orbital(y4, z4, 0) // 2 * 4 + local, rows)
    right_ref[...] = exact_rows(row // 8 * 4 + local, rows)


def first_stage_kernel(right_ref, left_ref, out_ref):
    for target in range(4):
        out_ref[target, 0:128, :] = right_ref[...]
        out_ref[target, 128:160, :] = left_ref[32 * target : 32 * target + 32, :]


def second_stage_kernel(in_ref, out_ref):
    for target in range(4):
        for source in range(4):
            out_ref[target, 128 * source : 128 * source + 128, :] = in_ref[source, 0:128, :]
            at = 128 + 8 * target
            out_ref[target, 512 + 8 * source : 520 + 8 * source, :] = in_ref[source, at : at + 8, :]


def density_kernel(where, occ_ref, left_ref, own_ref, other_ref, vir_ref, out_ref, coulomb, total):
    core = where[3]
    down = jnp.broadcast_to(vir_ref[...], (512, 512))
    total[...] = down.T + down
    coulomb[...] = jnp.zeros_like(coulomb)

    def own(second):
        return own_ref[second, 0:512, :]

    def other(second):
        at = pl.ds(pl.multiple_of(second * 128, 128), 128)
        return jnp.concatenate([other_ref[first, at, :] for first in range(4)])

    for second in range(4):
        left = jnp.concatenate([left_ref[:, second * 4 + first].reshape(128, 512) for first in range(4)]).T
        coulomb[0] += jnp.dot(left, own(second), preferred_element_type=jnp.float32)
        coulomb[1] += jnp.dot(left, other(second), preferred_element_type=jnp.float32)

    amplitudes = []
    for pick in range(2):
        plain = coulomb[pick]
        flipped = plain.T
        denominator = total[...] - occ_ref[where[0]] - occ_ref[where[1 + pick]]
        amplitudes.append(((2.0 * flipped - plain) / denominator).astype(jnp.bfloat16))

    for second in range(4):
        term = jnp.dot(own(second), amplitudes[0], preferred_element_type=jnp.float32)
        term += jnp.dot(other(second), amplitudes[1], preferred_element_type=jnp.float32)
        term = term.astype(jnp.bfloat16)
        for first in range(4):
            y4, z4 = jnp.where(core == 0, first, second), jnp.where(core == 0, second, first)
            for xl in range(2):
                for yb in range(2):
                    share = xl * 8 + (y4 // 2) * 4 + yb * 2 + y4 % 2
                    at = first * 128 + xl * 64 + yb * 32
                    out_ref[share, pl.ds(pl.multiple_of(z4 * 32, 32), 32), :] = term[at : at + 32]


def sum_kernel(shares, out_ref):
    total = shares[0].astype(jnp.float32)
    for source in range(1, 16):
        total += shares[source].astype(jnp.float32)
    row = lax.broadcasted_iota(jnp.int32, (128, 128), 0)
    local, xh, zb, z4, core = row % 4, (row // 4) % 2, (row // 8) % 2, (row // 16) % 4, row // 64
    source_row = (((z4 * 2 + xh) * 2 + zb) * 2 + core) * 4 + local
    out_ref[...] = exact_rows(source_row, total.astype(jnp.bfloat16))


def call(kernel, shapes, specs, scratch=(), flops=0):
    return pl.pallas_call(
        kernel,
        out_shape=[jax.ShapeDtypeStruct(shape, jnp.bfloat16) for shape in shapes],
        in_specs=specs,
        out_specs=[VMEM] * len(shapes),
        scratch_shapes=list(scratch),
        compiler_params=pltpu.CompilerParams(vmem_limit_bytes=24 * MIB),
        cost_estimate=pl.CostEstimate(flops=flops, bytes_accessed=2 * MIB, transcendentals=0),
    )


def device(**at):
    index = 0
    for name, size in zip(AXES, SIZES):
        index = index * size + at[name]
    return index


def places():
    for index in range(512):
        at, rest = {}, index
        for name, size in zip(AXES[::-1], SIZES[::-1]):
            rest, at[name] = divmod(rest, size)
        yield index, at


def lines(core_along_y):
    groups = []
    for _, at in places():
        axis = "y4" if at["c"] == core_along_y else "z4"
        if at[axis] == 0:
            groups.append([device(**{**at, axis: k}) for k in range(4)])
    return groups


def exchange(rows, axes, groups=None):
    return lax.all_to_all(rows, axes, split_axis=0, concat_axis=0, axis_index_groups=groups, tiled=True)


def to_place():
    return [
        (index, device(**{**at, "xl": at["z4"] // 2, "yb": at["z4"] % 2, "z4": at["xl"] * 2 + at["yb"]}))
        for index, at in places()
    ]


def body(half_ints, vir_coef, occ_energy, vir_energy):
    xl, y4, yb, c, z4, zb, xh = (lax.axis_index(a) for a in AXES)
    pair = (((xl * 2 + yb) * 2 + xh) * 2 + zb) * 2
    where = jnp.stack([left_orbital(y4, z4, c), pair + c, pair + 1 - c, c])
    flattened = half_ints.reshape(128, 576)
    got = lax.ppermute(flattened, "c", [(0, 1), (1, 0)])
    (rows,) = call(own_rows_kernel, [(64, 512)], [SMEM, VMEM, VMEM])(where, flattened, vir_coef)
    to_left, to_right = call(three_index_kernel, [(128, 512)] * 2, [SMEM, VMEM, VMEM, VMEM])(where, rows, got, vir_coef)
    right = exchange(to_right.reshape(16, 8, 512), COMPACT)
    (pieces,) = call(first_stage_kernel, [(4, 160, 512)], [VMEM, VMEM])(right.reshape(128, 512), to_left)
    pieces = exchange(pieces, AXES, lines(0))
    (pieces,) = call(second_stage_kernel, [(4, 544, 512)], [VMEM])(pieces)
    own = exchange(pieces, AXES, lines(1))
    other = lax.ppermute(own, "c", [(0, 1), (1, 0)])
    left = jnp.broadcast_to(own[None, :, 512:], (16, 4, 32, 512)).reshape(16, 128, 512)
    left = exchange(left, COMPACT)
    (partial,) = call(
        density_kernel,
        [(16, 128, 512)],
        [SMEM, SMEM, VMEM, VMEM, VMEM, VMEM],
        [pltpu.VMEM((2, 512, 512), jnp.float32), pltpu.VMEM((512, 512), jnp.float32)],
        flops=4 * 512 * 1024 * 2048,
    )(where, occ_energy, left.reshape(16, 16, 8, 512), own, other, vir_energy.reshape(1, 512))
    shares = exchange(partial, COMPACT)
    (summed,) = call(sum_kernel, [(128, 512)], [VMEM])(shares)
    placed = lax.ppermute(summed, AXES, to_place())
    return placed.astype(jnp.float32).reshape(128, 1, 512)


def solution(mesh):
    fine = Mesh(mesh.devices.reshape(SIZES), AXES)
    return jax.shard_map(
        body,
        mesh=fine,
        in_specs=(P(AXES, None, None), P(), P(), P()),
        out_specs=P(("z4", "zb", "xh"), ("xl", "y4", "yb", "c"), None),
        check_vma=False,
    )
```

```python
import itertools

import jax
import jax.numpy as jnp
from jax import lax
from jax.experimental import pallas as pl
from jax.experimental.pallas import tpu as pltpu
from jax.sharding import Mesh
from jax.sharding import PartitionSpec as P


AXES = ("xl", "y4", "yb", "c", "z4", "zb", "xh")
SIZES = (2, 4, 2, 2, 4, 2, 2)
COMPACT = ("xl", "yb", "xh", "zb")
MIB = 1 << 20
VMEM = pl.BlockSpec(memory_space=pltpu.VMEM)
SMEM = pl.BlockSpec(memory_space=pltpu.SMEM)


def exact_rows(source_row, rows):
    wanted = lax.broadcasted_iota(jnp.int32, source_row.shape, 1)
    selection = (wanted == source_row).astype(jnp.bfloat16)
    return jnp.dot(selection, rows, preferred_element_type=jnp.float32).astype(jnp.bfloat16)


def left_orbital(y4, z4, c):
    return ((z4 // 2) * 8 + y4 * 2 + z4 % 2) * 2 + c


def kept_rows(core, half_ref, coef_ref):
    row = lax.broadcasted_iota(jnp.int32, (64, 128), 0)
    half_ints = exact_rows(row % 4 * 32 + row // 4 * 2 + core, half_ref[...])
    return jnp.dot(half_ints, coef_ref[...], preferred_element_type=jnp.float32).astype(jnp.bfloat16)


def own_rows_kernel(where, half_ref, coef_ref, out_ref):
    out_ref[...] = kept_rows(where[3], half_ref, coef_ref)


def three_index_kernel(where, own_ref, got_ref, coef_ref, left_ref, right_ref):
    core = where[3]
    rows = jnp.concatenate([own_ref[...], kept_rows(core, got_ref, coef_ref)])
    row = lax.broadcasted_iota(jnp.int32, (128, 128), 0)
    local, first, second = row % 4 + 64 * ((row // 4 + core) % 2), row // 32, (row // 8) % 4
    y4, z4 = jnp.where(core == 0, first, second), jnp.where(core == 0, second, first)
    left_ref[...] = exact_rows(left_orbital(y4, z4, 0) // 2 * 4 + local, rows)
    right_ref[...] = exact_rows(row // 8 * 4 + local, rows)


def first_stage_kernel(right_ref, left_ref, out_ref):
    for target in range(4):
        out_ref[target, 0:128, :] = right_ref[...]
        out_ref[target, 128:160, :] = left_ref[32 * target : 32 * target + 32, :]


def second_stage_kernel(in_ref, out_ref):
    for target in range(4):
        for source in range(4):
            out_ref[target, 128 * source : 128 * source + 128, :] = in_ref[source, 0:128, :]
            at = 128 + 8 * target
            out_ref[target, 512 + 8 * source : 520 + 8 * source, :] = in_ref[source, at : at + 8, :]


def density_kernel(where, occ_ref, left_ref, own_ref, other_ref, vir_ref, out_ref, coulomb, total):
    core = where[3]
    down = jnp.broadcast_to(vir_ref[...], (512, 512))
    total[...] = down.T + down
    coulomb[...] = jnp.zeros_like(coulomb)

    def own(second):
        return own_ref[second, 0:512, :]

    def other(second):
        at = pl.ds(pl.multiple_of(second * 128, 128), 128)
        return jnp.concatenate([other_ref[first, at, :] for first in range(4)])

    for second in range(4):
        left = jnp.concatenate([left_ref[:, second * 4 + first].reshape(128, 512) for first in range(4)]).T
        coulomb[0] += jnp.dot(left, own(second), preferred_element_type=jnp.float32)
        coulomb[1] += jnp.dot(left, other(second), preferred_element_type=jnp.float32)

    amplitudes = []
    for pick in range(2):
        plain = coulomb[pick]
        flipped = plain.T
        denominator = total[...] - occ_ref[where[0]] - occ_ref[where[1 + pick]]
        amplitudes.append(((2.0 * flipped - plain) / denominator).astype(jnp.bfloat16))

    for second in range(4):
        term = jnp.dot(own(second), amplitudes[0], preferred_element_type=jnp.float32)
        term += jnp.dot(other(second), amplitudes[1], preferred_element_type=jnp.float32)
        term = term.astype(jnp.bfloat16)
        for first in range(4):
            y4, z4 = jnp.where(core == 0, first, second), jnp.where(core == 0, second, first)
            for xl in range(2):
                for yb in range(2):
                    share = xl * 8 + (y4 // 2) * 4 + (yb ^ (y4 // 2)) * 2 + y4 % 2
                    at = first * 128 + xl * 64 + yb * 32
                    out_ref[share, pl.ds(pl.multiple_of(z4 * 32, 32), 32), :] = term[at : at + 32]


def sum_kernel(shares, out_ref):
    total = shares[0].astype(jnp.float32)
    for source in range(1, 16):
        total += shares[source].astype(jnp.float32)
    row = lax.broadcasted_iota(jnp.int32, (128, 128), 0)
    local, xh, zb, z4, core = row % 4, (row // 4) % 2, (row // 8) % 2, (row // 16) % 4, row // 64
    source_row = (((z4 * 2 + xh) * 2 + (zb ^ (z4 // 2))) * 2 + core) * 4 + local
    out_ref[...] = exact_rows(source_row, total.astype(jnp.bfloat16))


def call(kernel, shapes, specs, scratch=(), flops=0):
    return pl.pallas_call(
        kernel,
        out_shape=[jax.ShapeDtypeStruct(shape, jnp.bfloat16) for shape in shapes],
        in_specs=specs,
        out_specs=[VMEM] * len(shapes),
        scratch_shapes=list(scratch),
        compiler_params=pltpu.CompilerParams(vmem_limit_bytes=24 * MIB),
        cost_estimate=pl.CostEstimate(flops=flops, bytes_accessed=2 * MIB, transcendentals=0),
    )


def device(**at):
    index = 0
    for name, size in zip(AXES, SIZES):
        index = index * size + at[name]
    return index


def places():
    for index in range(512):
        at, rest = {}, index
        for name, size in zip(AXES[::-1], SIZES[::-1]):
            rest, at[name] = divmod(rest, size)
        yield index, at


def on_line(at, axis, k):
    bit = {"y4": "yb", "z4": "zb"}[axis]
    return device(**{**at, axis: k, bit: at[bit] ^ k // 2})


def lines(core_along_y):
    groups = []
    for _, at in places():
        axis = "y4" if at["c"] == core_along_y else "z4"
        if at[axis] == 0:
            groups.append([on_line(at, axis, k) for k in range(4)])
    return groups


def compact():
    groups = []
    for y4, c, z4 in itertools.product(range(4), range(2), range(4)):
        groups.append(
            [
                device(xl=xl, y4=y4, yb=y ^ y4 // 2, c=c, z4=z4, zb=z ^ z4 // 2, xh=xh)
                for xl, y, xh, z in itertools.product(range(2), repeat=4)
            ]
        )
    return groups


def exchange(rows, axes, groups=None):
    return lax.all_to_all(rows, axes, split_axis=0, concat_axis=0, axis_index_groups=groups, tiled=True)


def to_place():
    return [
        (index, device(**{**at, "xl": at["z4"] // 2, "yb": at["z4"] % 2, "z4": at["xl"] * 2 + at["yb"]}))
        for index, at in places()
    ]


def body(half_ints, vir_coef, occ_energy, vir_energy):
    xl, y4, yb, c, z4, zb, xh = (lax.axis_index(a) for a in AXES)
    pair = (((xl * 2 + (yb ^ y4 // 2)) * 2 + xh) * 2 + (zb ^ z4 // 2)) * 2
    where = jnp.stack([left_orbital(y4, z4, c), pair + c, pair + 1 - c, c])
    flattened = half_ints.reshape(128, 576)
    got = lax.ppermute(flattened, "c", [(0, 1), (1, 0)])
    (rows,) = call(own_rows_kernel, [(64, 512)], [SMEM, VMEM, VMEM])(where, flattened, vir_coef)
    to_left, to_right = call(three_index_kernel, [(128, 512)] * 2, [SMEM, VMEM, VMEM, VMEM])(where, rows, got, vir_coef)
    right = exchange(to_right.reshape(16, 8, 512), AXES, compact())
    (pieces,) = call(first_stage_kernel, [(4, 160, 512)], [VMEM, VMEM])(right.reshape(128, 512), to_left)
    pieces = exchange(pieces, AXES, lines(0))
    (pieces,) = call(second_stage_kernel, [(4, 544, 512)], [VMEM])(pieces)
    own = exchange(pieces, AXES, lines(1))
    other = lax.ppermute(own, "c", [(0, 1), (1, 0)])
    left = jnp.broadcast_to(own[None, :, 512:], (16, 4, 32, 512)).reshape(16, 128, 512)
    left = exchange(left, AXES, compact())
    (partial,) = call(
        density_kernel,
        [(16, 128, 512)],
        [SMEM, SMEM, VMEM, VMEM, VMEM, VMEM],
        [pltpu.VMEM((2, 512, 512), jnp.float32), pltpu.VMEM((512, 512), jnp.float32)],
        flops=4 * 512 * 1024 * 2048,
    )(where, occ_energy, left.reshape(16, 16, 8, 512), own, other, vir_energy.reshape(1, 512))
    shares = exchange(partial, COMPACT)
    (summed,) = call(sum_kernel, [(128, 512)], [VMEM])(shares)
    placed = lax.ppermute(summed, AXES, to_place())
    return placed.astype(jnp.float32).reshape(128, 1, 512)


def solution(mesh):
    fine = Mesh(mesh.devices.reshape(SIZES), AXES)
    return jax.shard_map(
        body,
        mesh=fine,
        in_specs=(P(AXES, None, None), P(), P(), P()),
        out_specs=P(("z4", "zb", "xh"), ("xl", "y4", "yb", "c"), None),
        check_vma=False,
    )
```

```python
import itertools

import jax
import jax.numpy as jnp
from jax import lax
from jax.experimental import pallas as pl
from jax.experimental.pallas import tpu as pltpu
from jax.sharding import Mesh
from jax.sharding import PartitionSpec as P


AXES = ("xl", "y4", "yb", "c", "z4", "zb", "xh")
SIZES = (2, 4, 2, 2, 4, 2, 2)
COMPACT = ("xl", "yb", "xh", "zb")
MIB = 1 << 20
VMEM = pl.BlockSpec(memory_space=pltpu.VMEM)
SMEM = pl.BlockSpec(memory_space=pltpu.SMEM)


def exact_rows(source_row, rows):
    wanted = lax.broadcasted_iota(jnp.int32, source_row.shape, 1)
    selection = (wanted == source_row).astype(jnp.bfloat16)
    return jnp.dot(selection, rows, preferred_element_type=jnp.float32).astype(jnp.bfloat16)


def left_orbital(y4, z4, c):
    return ((z4 // 2) * 8 + y4 * 2 + z4 % 2) * 2 + c


def kept_rows(core, half_ref, coef_ref):
    row = lax.broadcasted_iota(jnp.int32, (64, 128), 0)
    half_ints = exact_rows(row % 4 * 32 + row // 4 * 2 + core, half_ref[...])
    return jnp.dot(half_ints, coef_ref[...], preferred_element_type=jnp.float32).astype(jnp.bfloat16)


def own_rows_kernel(where, half_ref, coef_ref, out_ref):
    out_ref[...] = kept_rows(where[3], half_ref, coef_ref)


def three_index_kernel(where, own_ref, got_ref, coef_ref, left_ref, right_ref):
    core = where[3]
    rows = jnp.concatenate([own_ref[...], kept_rows(core, got_ref, coef_ref)])
    row = lax.broadcasted_iota(jnp.int32, (128, 128), 0)
    local, first, second = row % 4 + 64 * ((row // 4 + core) % 2), row // 32, (row // 8) % 4
    y4, z4 = jnp.where(core == 0, first, second), jnp.where(core == 0, second, first)
    left_ref[...] = exact_rows(left_orbital(y4, z4, 0) // 2 * 4 + local, rows)
    right_ref[...] = exact_rows(row // 8 * 4 + local, rows)


def first_stage_kernel(right_ref, left_ref, out_ref):
    for target in range(4):
        out_ref[target, 0:128, :] = right_ref[...]
        out_ref[target, 128:160, :] = left_ref[32 * target : 32 * target + 32, :]


def second_stage_kernel(in_ref, out_ref):
    for target in range(4):
        for source in range(4):
            out_ref[target, 128 * source : 128 * source + 128, :] = in_ref[source, 0:128, :]
            at = 128 + 8 * target
            out_ref[target, 512 + 8 * source : 520 + 8 * source, :] = in_ref[source, at : at + 8, :]


def density_kernel(where, occ_ref, left_ref, own_ref, other_ref, vir_ref, out_ref, coulomb, total):
    core = where[3]
    down = jnp.broadcast_to(vir_ref[...], (512, 512))
    total[...] = down.T + down
    coulomb[...] = jnp.zeros_like(coulomb)

    def own(second):
        return own_ref[second, 0:512, :]

    def other(second):
        at = pl.ds(pl.multiple_of(second * 128, 128), 128)
        return jnp.concatenate([other_ref[first, at, :] for first in range(4)])

    for second in range(4):
        left = jnp.concatenate([left_ref[:, second * 4 + first].reshape(128, 512) for first in range(4)]).T
        coulomb[0] += jnp.dot(left, own(second), preferred_element_type=jnp.float32)
        coulomb[1] += jnp.dot(left, other(second), preferred_element_type=jnp.float32)

    amplitudes = []
    for pick in range(2):
        plain = coulomb[pick]
        flipped = plain.T
        denominator = total[...] - occ_ref[where[0]] - occ_ref[where[1 + pick]]
        amplitudes.append(((2.0 * flipped - plain) / denominator).astype(jnp.bfloat16))

    for second in range(4):
        term = jnp.dot(own(second), amplitudes[0], preferred_element_type=jnp.float32)
        term += jnp.dot(other(second), amplitudes[1], preferred_element_type=jnp.float32)
        term = term.astype(jnp.bfloat16)
        for first in range(4):
            y4, z4 = jnp.where(core == 0, first, second), jnp.where(core == 0, second, first)
            for xl in range(2):
                for yb in range(2):
                    share = xl * 8 + (y4 // 2) * 4 + (yb ^ (y4 // 2)) * 2 + ((y4 % 2) ^ xl ^ where[4])
                    at = first * 128 + xl * 64 + yb * 32
                    out_ref[share, pl.ds(pl.multiple_of(z4 * 32, 32), 32), :] = term[at : at + 32]


def sum_kernel(shares, out_ref):
    total = shares[0].astype(jnp.float32)
    for source in range(1, 16):
        total += shares[source].astype(jnp.float32)
    row = lax.broadcasted_iota(jnp.int32, (128, 128), 0)
    local, xh, zb, z4, core = row % 4, (row // 4) % 2, (row // 8) % 2, (row // 16) % 4, row // 64
    source_row = (((z4 * 2 + xh) * 2 + (zb ^ (z4 // 2))) * 2 + core) * 4 + local
    out_ref[...] = exact_rows(source_row, total.astype(jnp.bfloat16))


def call(kernel, shapes, specs, scratch=(), flops=0):
    return pl.pallas_call(
        kernel,
        out_shape=[jax.ShapeDtypeStruct(shape, jnp.bfloat16) for shape in shapes],
        in_specs=specs,
        out_specs=[VMEM] * len(shapes),
        scratch_shapes=list(scratch),
        compiler_params=pltpu.CompilerParams(vmem_limit_bytes=24 * MIB),
        cost_estimate=pl.CostEstimate(flops=flops, bytes_accessed=2 * MIB, transcendentals=0),
    )


def device(**at):
    index = 0
    for name, size in zip(AXES, SIZES):
        index = index * size + at[name]
    return index


def places():
    for index in range(512):
        at, rest = {}, index
        for name, size in zip(AXES[::-1], SIZES[::-1]):
            rest, at[name] = divmod(rest, size)
        yield index, at


def on_line(at, axis, k):
    bit = {"y4": "yb", "z4": "zb"}[axis]
    return device(**{**at, axis: k, bit: at[bit] ^ k // 2})


def lines(core_along_y):
    groups = []
    for _, at in places():
        axis = "y4" if at["c"] == core_along_y else "z4"
        if at[axis] == 0:
            groups.append([on_line(at, axis, k) for k in range(4)])
    return groups


def compact():
    groups = []
    for y4, c, z4 in itertools.product(range(4), range(2), range(4)):
        groups.append(
            [
                device(xl=xl, y4=y4, yb=y ^ y4 // 2, c=c, z4=z4, zb=z ^ z4 // 2, xh=xh)
                for xl, y, xh, z in itertools.product(range(2), repeat=4)
            ]
        )
    return groups


def exchange(rows, axes, groups=None):
    return lax.all_to_all(rows, axes, split_axis=0, concat_axis=0, axis_index_groups=groups, tiled=True)


def to_place():
    return [
        (
            index,
            device(
                **{
                    **at,
                    "xl": at["z4"] // 2,
                    "yb": at["z4"] % 2,
                    "z4": at["xl"] * 2 + at["yb"],
                    "zb": at["zb"] ^ at["xl"] ^ at["z4"] // 2,
                }
            ),
        )
        for index, at in places()
    ]


def body(half_ints, vir_coef, occ_energy, vir_energy):
    xl, y4, yb, c, z4, zb, xh = (lax.axis_index(a) for a in AXES)
    pair = (((xl * 2 + (yb ^ y4 // 2)) * 2 + xh) * 2 + (zb ^ z4 // 2)) * 2
    where = jnp.stack([left_orbital(y4, z4, c), pair + c, pair + 1 - c, c, z4 // 2])
    flattened = half_ints.reshape(128, 576)
    got = lax.ppermute(flattened, "c", [(0, 1), (1, 0)])
    (rows,) = call(own_rows_kernel, [(64, 512)], [SMEM, VMEM, VMEM])(where, flattened, vir_coef)
    to_left, to_right = call(three_index_kernel, [(128, 512)] * 2, [SMEM, VMEM, VMEM, VMEM])(where, rows, got, vir_coef)
    right = exchange(to_right.reshape(16, 8, 512), AXES, compact())
    (pieces,) = call(first_stage_kernel, [(4, 160, 512)], [VMEM, VMEM])(right.reshape(128, 512), to_left)
    pieces = exchange(pieces, AXES, lines(0))
    (pieces,) = call(second_stage_kernel, [(4, 544, 512)], [VMEM])(pieces)
    own = exchange(pieces, AXES, lines(1))
    other = lax.ppermute(own, "c", [(0, 1), (1, 0)])
    left = jnp.broadcast_to(own[None, :, 512:], (16, 4, 32, 512)).reshape(16, 128, 512)
    left = exchange(left, AXES, compact())
    (partial,) = call(
        density_kernel,
        [(16, 128, 512)],
        [SMEM, SMEM, VMEM, VMEM, VMEM, VMEM],
        [pltpu.VMEM((2, 512, 512), jnp.float32), pltpu.VMEM((512, 512), jnp.float32)],
        flops=4 * 512 * 1024 * 2048,
    )(where, occ_energy, left.reshape(16, 16, 8, 512), own, other, vir_energy.reshape(1, 512))
    shares = exchange(partial, COMPACT)
    (summed,) = call(sum_kernel, [(128, 512)], [VMEM])(shares)
    placed = lax.ppermute(summed, AXES, to_place())
    return placed.astype(jnp.float32).reshape(128, 1, 512)


def solution(mesh):
    fine = Mesh(mesh.devices.reshape(SIZES), AXES)
    return jax.shard_map(
        body,
        mesh=fine,
        in_specs=(P(AXES, None, None), P(), P(), P()),
        out_specs=P(("z4", "zb", "xh"), ("xl", "y4", "yb", "c"), None),
        check_vma=False,
    )
```

```python
import itertools

import jax
import jax.numpy as jnp
from jax import lax
from jax.experimental import pallas as pl
from jax.experimental.pallas import tpu as pltpu
from jax.sharding import Mesh
from jax.sharding import PartitionSpec as P


AXES = ("xl", "y4", "yb", "c", "z4", "zb", "xh")
SIZES = (2, 4, 2, 2, 4, 2, 2)
COMPACT = ("xl", "yb", "xh", "zb")
MIB = 1 << 20
VMEM = pl.BlockSpec(memory_space=pltpu.VMEM)
SMEM = pl.BlockSpec(memory_space=pltpu.SMEM)


def exact_rows(source_row, rows):
    wanted = lax.broadcasted_iota(jnp.int32, source_row.shape, 1)
    selection = (wanted == source_row).astype(jnp.bfloat16)
    return jnp.dot(selection, rows, preferred_element_type=jnp.float32).astype(jnp.bfloat16)


def left_orbital(y4, z4, c):
    return ((z4 // 2) * 8 + y4 * 2 + z4 % 2) * 2 + c


def kept_rows(core, half_ref, coef_ref):
    row = lax.broadcasted_iota(jnp.int32, (64, 128), 0)
    half_ints = exact_rows(row % 4 * 32 + row // 4 * 2 + core, half_ref[...])
    return jnp.dot(half_ints, coef_ref[...], preferred_element_type=jnp.float32).astype(jnp.bfloat16)


def own_rows_kernel(where, half_ref, coef_ref, out_ref, held_ref):
    held_ref[...] = coef_ref[...]
    out_ref[...] = kept_rows(where[3], half_ref, coef_ref)


def three_index_kernel(where, own_ref, got_ref, coef_ref, left_ref, right_ref):
    core = where[3]
    rows = jnp.concatenate([own_ref[...], kept_rows(core, got_ref, coef_ref)])
    row = lax.broadcasted_iota(jnp.int32, (128, 128), 0)
    local, first, second = row % 4 + 64 * ((row // 4 + core) % 2), row // 32, (row // 8) % 4
    y4, z4 = jnp.where(core == 0, first, second), jnp.where(core == 0, second, first)
    left_ref[...] = exact_rows(left_orbital(y4, z4, 0) // 2 * 4 + local, rows)
    right_ref[...] = exact_rows(row // 8 * 4 + local, rows)


def first_stage_kernel(right_ref, left_ref, out_ref):
    for target in range(4):
        out_ref[target, 0:128, :] = right_ref[...]
        out_ref[target, 128:160, :] = left_ref[32 * target : 32 * target + 32, :]


def second_stage_kernel(in_ref, out_ref):
    for target in range(4):
        for source in range(4):
            out_ref[target, 128 * source : 128 * source + 128, :] = in_ref[source, 0:128, :]
            at = 128 + 8 * target
            out_ref[target, 512 + 8 * source : 520 + 8 * source, :] = in_ref[source, at : at + 8, :]


def density_kernel(where, occ_ref, left_ref, own_ref, other_ref, vir_ref, out_ref, coulomb, total):
    core = where[3]
    down = jnp.broadcast_to(vir_ref[...], (512, 512))
    total[...] = down.T + down
    coulomb[...] = jnp.zeros_like(coulomb)

    def own(second):
        return own_ref[second, 0:512, :]

    def other(second):
        at = pl.ds(pl.multiple_of(second * 128, 128), 128)
        return jnp.concatenate([other_ref[first, at, :] for first in range(4)])

    for second in range(4):
        left = jnp.concatenate([left_ref[:, second * 4 + first].reshape(128, 512) for first in range(4)]).T
        coulomb[0] += jnp.dot(left, own(second), preferred_element_type=jnp.float32)
        coulomb[1] += jnp.dot(left, other(second), preferred_element_type=jnp.float32)

    amplitudes = []
    for pick in range(2):
        plain = coulomb[pick]
        flipped = plain.T
        denominator = total[...] - occ_ref[where[0]] - occ_ref[where[1 + pick]]
        amplitudes.append(((2.0 * flipped - plain) / denominator).astype(jnp.bfloat16))

    for second in range(4):
        term = jnp.dot(own(second), amplitudes[0], preferred_element_type=jnp.float32)
        term += jnp.dot(other(second), amplitudes[1], preferred_element_type=jnp.float32)
        term = term.astype(jnp.bfloat16)
        for first in range(4):
            y4, z4 = jnp.where(core == 0, first, second), jnp.where(core == 0, second, first)
            for xl in range(2):
                for yb in range(2):
                    share = xl * 8 + (y4 // 2) * 4 + (yb ^ (y4 // 2)) * 2 + ((y4 % 2) ^ xl ^ where[4])
                    at = first * 128 + xl * 64 + yb * 32
                    out_ref[share, pl.ds(pl.multiple_of(z4 * 32, 32), 32), :] = term[at : at + 32]


def sum_kernel(shares, out_ref):
    total = shares[0].astype(jnp.float32)
    for source in range(1, 16):
        total += shares[source].astype(jnp.float32)
    row = lax.broadcasted_iota(jnp.int32, (128, 128), 0)
    local, xh, zb, z4, core = row % 4, (row // 4) % 2, (row // 8) % 2, (row // 16) % 4, row // 64
    source_row = (((z4 * 2 + xh) * 2 + (zb ^ (z4 // 2))) * 2 + core) * 4 + local
    out_ref[...] = exact_rows(source_row, total.astype(jnp.bfloat16))


def call(kernel, shapes, specs, scratch=(), flops=0):
    return pl.pallas_call(
        kernel,
        out_shape=[jax.ShapeDtypeStruct(shape, jnp.bfloat16) for shape in shapes],
        in_specs=specs,
        out_specs=[VMEM] * len(shapes),
        scratch_shapes=list(scratch),
        compiler_params=pltpu.CompilerParams(vmem_limit_bytes=24 * MIB),
        cost_estimate=pl.CostEstimate(flops=flops, bytes_accessed=2 * MIB, transcendentals=0),
    )


def device(**at):
    index = 0
    for name, size in zip(AXES, SIZES):
        index = index * size + at[name]
    return index


def places():
    for index in range(512):
        at, rest = {}, index
        for name, size in zip(AXES[::-1], SIZES[::-1]):
            rest, at[name] = divmod(rest, size)
        yield index, at


def on_line(at, axis, k):
    bit = {"y4": "yb", "z4": "zb"}[axis]
    return device(**{**at, axis: k, bit: at[bit] ^ k // 2})


def lines(core_along_y):
    groups = []
    for _, at in places():
        axis = "y4" if at["c"] == core_along_y else "z4"
        if at[axis] == 0:
            groups.append([on_line(at, axis, k) for k in range(4)])
    return groups


def compact():
    groups = []
    for y4, c, z4 in itertools.product(range(4), range(2), range(4)):
        groups.append(
            [
                device(xl=xl, y4=y4, yb=y ^ y4 // 2, c=c, z4=z4, zb=z ^ z4 // 2, xh=xh)
                for xl, y, xh, z in itertools.product(range(2), repeat=4)
            ]
        )
    return groups


def exchange(rows, axes, groups=None):
    return lax.all_to_all(rows, axes, split_axis=0, concat_axis=0, axis_index_groups=groups, tiled=True)


def to_place():
    return [
        (
            index,
            device(
                **{
                    **at,
                    "xl": at["z4"] // 2,
                    "yb": at["z4"] % 2,
                    "z4": at["xl"] * 2 + at["yb"],
                    "zb": at["zb"] ^ at["xl"] ^ at["z4"] // 2,
                }
            ),
        )
        for index, at in places()
    ]


def body(half_ints, vir_coef, occ_energy, vir_energy):
    xl, y4, yb, c, z4, zb, xh = (lax.axis_index(a) for a in AXES)
    pair = (((xl * 2 + (yb ^ y4 // 2)) * 2 + xh) * 2 + (zb ^ z4 // 2)) * 2
    where = jnp.stack([left_orbital(y4, z4, c), pair + c, pair + 1 - c, c, z4 // 2])
    flattened = half_ints.reshape(128, 576)
    got = lax.ppermute(flattened, "c", [(0, 1), (1, 0)])
    rows, held = call(own_rows_kernel, [(64, 512), (576, 512)], [SMEM, VMEM, VMEM])(where, flattened, vir_coef)
    to_left, to_right = call(three_index_kernel, [(128, 512)] * 2, [SMEM, VMEM, VMEM, VMEM])(where, rows, got, held)
    right = exchange(to_right.reshape(16, 8, 512), AXES, compact())
    (pieces,) = call(first_stage_kernel, [(4, 160, 512)], [VMEM, VMEM])(right.reshape(128, 512), to_left)
    pieces = exchange(pieces, AXES, lines(0))
    (pieces,) = call(second_stage_kernel, [(4, 544, 512)], [VMEM])(pieces)
    own = exchange(pieces, AXES, lines(1))
    other = lax.ppermute(own, "c", [(0, 1), (1, 0)])
    left = jnp.broadcast_to(own[None, :, 512:], (16, 4, 32, 512)).reshape(16, 128, 512)
    left = exchange(left, AXES, compact())
    (partial,) = call(
        density_kernel,
        [(16, 128, 512)],
        [SMEM, SMEM, VMEM, VMEM, VMEM, VMEM],
        [pltpu.VMEM((2, 512, 512), jnp.float32), pltpu.VMEM((512, 512), jnp.float32)],
        flops=4 * 512 * 1024 * 2048,
    )(where, occ_energy, left.reshape(16, 16, 8, 512), own, other, vir_energy.reshape(1, 512))
    shares = exchange(partial, COMPACT)
    (summed,) = call(sum_kernel, [(128, 512)], [VMEM])(shares)
    placed = lax.ppermute(summed, AXES, to_place())
    return placed.astype(jnp.float32).reshape(128, 1, 512)


def solution(mesh):
    fine = Mesh(mesh.devices.reshape(SIZES), AXES)
    return jax.shard_map(
        body,
        mesh=fine,
        in_specs=(P(AXES, None, None), P(), P(), P()),
        out_specs=P(("z4", "zb", "xh"), ("xl", "y4", "yb", "c"), None),
        check_vma=False,
    )
```

```python
import itertools

import jax
import jax.numpy as jnp
from jax import lax
from jax.experimental import pallas as pl
from jax.experimental.pallas import tpu as pltpu
from jax.sharding import Mesh
from jax.sharding import PartitionSpec as P


AXES = ("xl", "y4", "yb", "c", "z4", "zb", "xh")
SIZES = (2, 4, 2, 2, 4, 2, 2)
COMPACT = ("xl", "yb", "xh", "zb")
MIB = 1 << 20
VMEM = pl.BlockSpec(memory_space=pltpu.VMEM)
SMEM = pl.BlockSpec(memory_space=pltpu.SMEM)
ANY = pl.BlockSpec(memory_space=pl.ANY)


def exact_rows(source_row, rows):
    wanted = lax.broadcasted_iota(jnp.int32, source_row.shape, 1)
    selection = (wanted == source_row).astype(jnp.bfloat16)
    return jnp.dot(selection, rows, preferred_element_type=jnp.float32).astype(jnp.bfloat16)


def left_orbital(y4, z4, c):
    return ((z4 // 2) * 8 + y4 * 2 + z4 % 2) * 2 + c


def kept_rows(core, half_ref, coef_ref):
    row = lax.broadcasted_iota(jnp.int32, (64, 128), 0)
    half_ints = exact_rows(row % 4 * 32 + row // 4 * 2 + core, half_ref[...])
    return jnp.dot(half_ints, coef_ref[...], preferred_element_type=jnp.float32).astype(jnp.bfloat16)


def own_rows_kernel(where, half_ref, coef_ref, out_ref, held_ref):
    held_ref[...] = coef_ref[...]
    out_ref[...] = kept_rows(where[3], half_ref, coef_ref)


def three_index_kernel(where, own_ref, got_ref, coef_ref, left_ref, right_ref):
    core = where[3]
    rows = jnp.concatenate([own_ref[...], kept_rows(core, got_ref, coef_ref)])
    row = lax.broadcasted_iota(jnp.int32, (128, 128), 0)
    local, first, second = row % 4 + 64 * ((row // 4 + core) % 2), row // 32, (row // 8) % 4
    y4, z4 = jnp.where(core == 0, first, second), jnp.where(core == 0, second, first)
    left_ref[...] = exact_rows(left_orbital(y4, z4, 0) // 2 * 4 + local, rows)
    right_ref[...] = exact_rows(row // 8 * 4 + local, rows)


def first_stage_kernel(right_ref, left_ref, out_ref):
    for target in range(4):
        out_ref[target, 0:128, :] = right_ref[...]
        out_ref[target, 128:160, :] = left_ref[32 * target : 32 * target + 32, :]


def second_stage_kernel(in_ref, out_ref):
    for target in range(4):
        for source in range(4):
            out_ref[target, 128 * source : 128 * source + 128, :] = in_ref[source, 0:128, :]
            at = 128 + 8 * target
            out_ref[target, 512 + 8 * source : 520 + 8 * source, :] = in_ref[source, at : at + 8, :]


def density_kernel(where, occ_ref, left_ref, own_ref, other_in, vir_ref, out_ref, coulomb, total, other_ref, arrived):
    core = where[3]
    fetch = pltpu.make_async_copy(other_in, other_ref, arrived)
    fetch.start()
    down = jnp.broadcast_to(vir_ref[...], (512, 512))
    total[...] = down.T + down
    coulomb[...] = jnp.zeros_like(coulomb)
    fetch.wait()

    def own(second):
        return own_ref[second, 0:512, :]

    def other(second):
        at = pl.ds(pl.multiple_of(second * 128, 128), 128)
        return jnp.concatenate([other_ref[first, at, :] for first in range(4)])

    for second in range(4):
        left = jnp.concatenate([left_ref[:, second * 4 + first].reshape(128, 512) for first in range(4)]).T
        coulomb[0] += jnp.dot(left, own(second), preferred_element_type=jnp.float32)
        coulomb[1] += jnp.dot(left, other(second), preferred_element_type=jnp.float32)

    amplitudes = []
    for pick in range(2):
        plain = coulomb[pick]
        flipped = plain.T
        denominator = total[...] - occ_ref[where[0]] - occ_ref[where[1 + pick]]
        amplitudes.append(((2.0 * flipped - plain) / denominator).astype(jnp.bfloat16))

    for second in range(4):
        term = jnp.dot(own(second), amplitudes[0], preferred_element_type=jnp.float32)
        term += jnp.dot(other(second), amplitudes[1], preferred_element_type=jnp.float32)
        term = term.astype(jnp.bfloat16)
        for first in range(4):
            y4, z4 = jnp.where(core == 0, first, second), jnp.where(core == 0, second, first)
            for xl in range(2):
                for yb in range(2):
                    share = xl * 8 + (y4 // 2) * 4 + (yb ^ (y4 // 2)) * 2 + ((y4 % 2) ^ xl ^ where[4])
                    at = first * 128 + xl * 64 + yb * 32
                    out_ref[share, pl.ds(pl.multiple_of(z4 * 32, 32), 32), :] = term[at : at + 32]


def sum_kernel(shares, out_ref):
    total = shares[0].astype(jnp.float32)
    for source in range(1, 16):
        total += shares[source].astype(jnp.float32)
    row = lax.broadcasted_iota(jnp.int32, (128, 128), 0)
    local, xh, zb, z4, core = row % 4, (row // 4) % 2, (row // 8) % 2, (row // 16) % 4, row // 64
    source_row = (((z4 * 2 + xh) * 2 + (zb ^ (z4 // 2))) * 2 + core) * 4 + local
    out_ref[...] = exact_rows(source_row, total.astype(jnp.bfloat16))


def call(kernel, shapes, specs, scratch=(), flops=0, vmem=24):
    return pl.pallas_call(
        kernel,
        out_shape=[jax.ShapeDtypeStruct(shape, jnp.bfloat16) for shape in shapes],
        in_specs=specs,
        out_specs=[VMEM] * len(shapes),
        scratch_shapes=list(scratch),
        compiler_params=pltpu.CompilerParams(vmem_limit_bytes=vmem * MIB),
        cost_estimate=pl.CostEstimate(flops=flops, bytes_accessed=2 * MIB, transcendentals=0),
    )


def device(**at):
    index = 0
    for name, size in zip(AXES, SIZES):
        index = index * size + at[name]
    return index


def places():
    for index in range(512):
        at, rest = {}, index
        for name, size in zip(AXES[::-1], SIZES[::-1]):
            rest, at[name] = divmod(rest, size)
        yield index, at


def on_line(at, axis, k):
    bit = {"y4": "yb", "z4": "zb"}[axis]
    return device(**{**at, axis: k, bit: at[bit] ^ k // 2})


def lines(core_along_y):
    groups = []
    for _, at in places():
        axis = "y4" if at["c"] == core_along_y else "z4"
        if at[axis] == 0:
            groups.append([on_line(at, axis, k) for k in range(4)])
    return groups


def compact():
    groups = []
    for y4, c, z4 in itertools.product(range(4), range(2), range(4)):
        groups.append(
            [
                device(xl=xl, y4=y4, yb=y ^ y4 // 2, c=c, z4=z4, zb=z ^ z4 // 2, xh=xh)
                for xl, y, xh, z in itertools.product(range(2), repeat=4)
            ]
        )
    return groups


def exchange(rows, axes, groups=None):
    return lax.all_to_all(rows, axes, split_axis=0, concat_axis=0, axis_index_groups=groups, tiled=True)


def to_place():
    return [
        (
            index,
            device(
                **{
                    **at,
                    "xl": at["z4"] // 2,
                    "yb": at["z4"] % 2,
                    "z4": at["xl"] * 2 + at["yb"],
                    "zb": at["zb"] ^ at["xl"] ^ at["z4"] // 2,
                }
            ),
        )
        for index, at in places()
    ]


def body(half_ints, vir_coef, occ_energy, vir_energy):
    xl, y4, yb, c, z4, zb, xh = (lax.axis_index(a) for a in AXES)
    pair = (((xl * 2 + (yb ^ y4 // 2)) * 2 + xh) * 2 + (zb ^ z4 // 2)) * 2
    where = jnp.stack([left_orbital(y4, z4, c), pair + c, pair + 1 - c, c, z4 // 2])
    flattened = half_ints.reshape(128, 576)
    got = lax.ppermute(flattened, "c", [(0, 1), (1, 0)])
    rows, held = call(own_rows_kernel, [(64, 512), (576, 512)], [SMEM, VMEM, VMEM])(where, flattened, vir_coef)
    to_left, to_right = call(three_index_kernel, [(128, 512)] * 2, [SMEM, VMEM, VMEM, VMEM])(where, rows, got, held)
    right = exchange(to_right.reshape(16, 8, 512), AXES, compact())
    (pieces,) = call(first_stage_kernel, [(4, 160, 512)], [VMEM, VMEM])(right.reshape(128, 512), to_left)
    pieces = exchange(pieces, AXES, lines(0))
    (pieces,) = call(second_stage_kernel, [(4, 544, 512)], [VMEM])(pieces)
    own = exchange(pieces, AXES, lines(1))
    other = lax.ppermute(own, "c", [(0, 1), (1, 0)])
    left = jnp.broadcast_to(own[None, :, 512:], (16, 4, 32, 512)).reshape(16, 128, 512)
    left = exchange(left, AXES, compact())
    (partial,) = call(
        density_kernel,
        [(16, 128, 512)],
        [SMEM, SMEM, VMEM, VMEM, ANY, VMEM],
        [
            pltpu.VMEM((2, 512, 512), jnp.float32),
            pltpu.VMEM((512, 512), jnp.float32),
            pltpu.VMEM((4, 544, 512), jnp.bfloat16),
            pltpu.SemaphoreType.DMA,
        ],
        flops=4 * 512 * 1024 * 2048,
        vmem=58,
    )(where, occ_energy, left.reshape(16, 16, 8, 512), own, other, vir_energy.reshape(1, 512))
    shares = exchange(partial, COMPACT)
    (summed,) = call(sum_kernel, [(128, 512)], [VMEM])(shares)
    placed = lax.ppermute(summed, AXES, to_place())
    return placed.astype(jnp.float32).reshape(128, 1, 512)


def solution(mesh):
    fine = Mesh(mesh.devices.reshape(SIZES), AXES)
    return jax.shard_map(
        body,
        mesh=fine,
        in_specs=(P(AXES, None, None), P(), P(), P()),
        out_specs=P(("z4", "zb", "xh"), ("xl", "y4", "yb", "c"), None),
        check_vma=False,
    )
```
